128 devices in a mesh: dom: 64 (over x, z, y), sub: 2 (over core).
Axes of the slice: x: 4, y: 4, z: 4, core: 2. Of those that a mesh axis runs over, the one named last changes fastest.
Arguments:
- a_blocks: bfloat16 [8192, 8, 128, 128], P(('dom', 'sub')), may hold values from -6 to 6
- nbr_offset: int32 [8192, 8], P(('dom', 'sub')), may hold values from -3 to 3
- nbr_count: int32 [8192], P(('dom', 'sub')), may hold values from 4 to 8
- prolong: bfloat16 [8192, 128, 128], P(('dom', 'sub')), may hold values from -0.5 to 0.5
- owner_start: int32 [128], replicated, may hold values from 0 to 8191, as said below
Outputs:
- coarse: float32 [2048, 7, 128, 128], P(('dom', 'sub'))
The draws below stay inside these ranges and needn't reach their ends.
Inputs may be any that keep to these rules, and one draw needn't show every extreme that they name: owner_start[0] = 0, owner_start[1] = 112, and owner_start[d] - d * 64 lies in 0 to 48 for every d.
All inputs are finite; a program needn't handle non-finite values.
Results may differ from the reference program's by a relative error of at most 0.0029.
Values may be sent and summed in bfloat16 or wider, within the bound.
A program may use at most 256 MiB of HBM per device.

```python
import jax
import jax.numpy as jnp
from jax import lax

B = 128
BC = 128
K = 8
W = 3
KC = 7
RB = 64
AD = 16
EMAX = 48
NF = 8192
NA = 2048


def draw_owner_start(key, part):
    count_owners = NF // RB
    shifts = jax.random.randint(key, (count_owners,), 0, EMAX + 1)
    owner_index = jnp.arange(count_owners, dtype=jnp.int32)
    shifts = jnp.where(owner_index == 0, 0, jnp.where(owner_index == 1, EMAX, shifts))
    return (owner_index * RB + shifts).astype(jnp.int32)


def with_ends(values, stream_key, smallest, high):
    shape = values.shape
    place = [jax.random.randint(jax.random.fold_in(stream_key, axis), (), 0, shape[axis]) for axis in range(len(shape))]
    values = values.at[tuple(place)].set(smallest)
    longest = shape.index(max(shape))
    place[longest] = (place[longest] + 1) % shape[longest]
    return values.at[tuple(place)].set(high)


def block_scale(stream_key, dims, pieces, smallest, top_value):
    def one(axis_at, shards_of):
        heights = jax.random.uniform(jax.random.fold_in(jax.random.fold_in(stream_key, 6), axis_at), (shards_of,), jnp.float32, smallest / len(pieces), top_value / len(pieces))
        return jnp.repeat(jnp.exp(heights), dims[axis_at] // shards_of).reshape((-1,) + (1,) * (len(dims) - axis_at - 1))

    loudness = one(*pieces[0])
    for cut in pieces[1:]:
        loudness = loudness * one(*cut)
    return loudness


def gaussian(rng, dims, scale, most, split=(), held_as=jnp.bfloat16):
    entries = jax.random.normal(rng, dims, jnp.float32) * scale
    if len(split) > 0:
        entries = block_scale(rng, dims, split, -0.22, 0.18) * entries
    return jnp.clip(entries, min=-most, max=most).astype(held_as)


def setup_inputs(seed: int = 0) -> dict:
    seeds = jax.random.split(jax.random.key(seed), 6)
    a_blocks = gaussian(seeds[0], (NF, K, B, B), 0.4, 6.0, ((0, 128),))
    nbr_offset = with_ends(jax.random.randint(seeds[1], (NF, K), 0 - W, W + 1), jax.random.fold_in(seeds[1], 1), 0 - W, W).astype(jnp.int32)
    nbr_count = with_ends(jax.random.randint(seeds[2], (NF,), K // 2, K + 1), jax.random.fold_in(seeds[2], 1), K // 2, K).astype(jnp.int32)
    prolong = gaussian(seeds[3], (NF, B, BC), B ** -0.5, 0.5, ((0, 128),))
    owner_start = draw_owner_start(jax.random.fold_in(seeds[5], 71), 0)
    return {"a_blocks": a_blocks, "nbr_offset": nbr_offset, "nbr_count": nbr_count, "prolong": prolong, "owner_start": owner_start}


def aggregate_ids(fine_ids, owner_start, total_rows):
    flat_ids = fine_ids.reshape(-1)
    bounds = jnp.concatenate([owner_start, jnp.full((1,), total_rows, jnp.int32)])
    owner_index = jnp.sum((owner_start[None, :] <= flat_ids[:, None]).astype(jnp.int32), axis=1) - 1
    first_row = bounds[owner_index]
    span_rows = bounds[owner_index + 1] - first_row
    local_ids = ((flat_ids - first_row) * AD) // span_rows
    return (owner_index * AD + local_ids).astype(jnp.int32).reshape(fine_ids.shape)


def galerkin_rows(blocks, window, offsets, counts, fine_ids, owner_start, total_rows):
    count_rows = blocks.shape[0]
    local_index = jnp.arange(count_rows, dtype=jnp.int32)[:, None] + W + offsets
    near_rows = window[local_index].astype(jnp.float32)
    products = jnp.einsum("rkab,rkbc->rkac", blocks.astype(jnp.float32), near_rows, precision=lax.Precision.HIGHEST)
    neighbour = fine_ids[:, None] + offsets
    is_valid = (jnp.arange(K, dtype=jnp.int32)[None, :] < counts[:, None]) & (neighbour >= 0) & (neighbour < total_rows)
    row_aggs = aggregate_ids(jnp.clip(fine_ids, 0, total_rows - 1), owner_start, total_rows)
    slot_index = aggregate_ids(jnp.clip(neighbour, 0, total_rows - 1), owner_start, total_rows) - row_aggs[:, None] + W
    select = ((slot_index[..., None] == jnp.arange(KC, dtype=jnp.int32)) & is_valid[..., None]).astype(jnp.float32)
    applied = jnp.einsum("rkq,rkac->rqac", select, products, precision=lax.Precision.HIGHEST).astype(jnp.bfloat16)
    own_rows = window[W:W + count_rows].astype(jnp.float32)
    return jnp.einsum("rbx,rqby->rqxy", own_rows, applied.astype(jnp.float32), precision=lax.Precision.HIGHEST)


def reference(a_blocks, nbr_offset, nbr_count, prolong, owner_start):
    padded = jnp.pad(prolong, ((W, W), (0, 0), (0, 0)))

    def add_group(group_index, coarse):
        first = (group_index * RB).astype(jnp.int32)
        blocks = lax.dynamic_slice_in_dim(a_blocks, first, RB, 0)
        offsets = lax.dynamic_slice_in_dim(nbr_offset, first, RB, 0)
        counts = lax.dynamic_slice_in_dim(nbr_count, first, RB, 0)
        window = lax.dynamic_slice_in_dim(padded, first, RB + 2 * W, 0)
        fine_ids = first + jnp.arange(RB, dtype=jnp.int32)
        terms = galerkin_rows(blocks, window, offsets, counts, fine_ids, owner_start, NF)
        row_aggs = aggregate_ids(fine_ids, owner_start, NF)
        return coarse.at[row_aggs].add(terms)

    start_value = jnp.zeros((NA, KC, BC, BC), jnp.float32)
    return lax.fori_loop(0, NF // RB, add_group, start_value)
```

```python
import functools

import jax
import jax.numpy as jnp
from jax import lax
from jax.experimental import pallas as pl
from jax.experimental.pallas import tpu as pltpu
from jax.sharding import PartitionSpec as P

BF = jnp.bfloat16
F32 = jnp.float32
W = 3
KC = 7
AD = 16
K = 8
B = 128
RB = 64
CHUNKS = (21, 24)
LAST_ROW = 24
FIRST_ROWS = 20
GROUP = 4
PAD = 7
OWN = AD * KC
EDGE = RB * 3 // 4 + 2 * W


def bases():
    at, out = OWN + PAD, []
    for size in CHUNKS:
        out.append(at)
        at += size + 2 * PAD
    return out, at


BASES, TRASH = bases()
BLOCKS = TRASH + KC


class Frame:
    def __init__(self, starts, dev, devices):
        def start_of(d):
            inner = starts[jnp.clip(d, 0, devices - 1)]
            return jnp.where(d >= devices, devices * RB, inner) - dev * RB

        self.initial = dev == 0
        self.final = dev >= devices - 1
        self.begin = [start_of(jnp.maximum(dev - 1, 0)), start_of(dev), start_of(dev + 1)]
        ends = [self.begin[1], self.begin[2], start_of(dev + 2)]
        self.length = [jnp.maximum(e - b, 1) for b, e in zip(self.begin, ends)]
        self.shift = jnp.where(dev >= devices, 0, self.begin[1])
        self.scale = [lax.div(jnp.int32(1 << 20), n) + 1 for n in self.length]

    def agg_start(self, owner, a):
        return self.begin[owner] + lax.shift_right_arithmetic(a * self.length[owner] + (AD - 1), 4)

    def fill(self, agg, count):
        def one(t, carry):
            i = t - W
            p0, p1, p2 = [i - b for b in self.begin]
            later = jnp.logical_or(p1 >= 0, self.initial)
            last = jnp.logical_and(p2 >= 0, jnp.logical_not(self.final))
            p = jnp.where(last, p2, jnp.where(later, p1, p0))
            m = jnp.where(last, self.scale[2], jnp.where(later, self.scale[1], self.scale[0]))
            o = jnp.where(last, 2 * AD, jnp.where(later, AD, 0))
            a = lax.shift_right_arithmetic(jnp.maximum(p, 0) * AD * m, 20)
            agg[t] = o + jnp.minimum(a, AD - 1)
            return carry

        lax.fori_loop(0, count, one, 0)

    def chunks(self, agg, visit):
        def one(a, carry):
            second, used, cut = carry
            i0 = jnp.maximum(self.agg_start(0, a), 0)
            i1 = self.agg_start(0, a + 1)
            low = agg[i0] - a + W
            n = agg[i1 + W + W - 1] - a + W - low + 1
            full = jnp.logical_or(used + n > CHUNKS[0], i0 >= LAST_ROW)
            over = jnp.logical_and(second == 0, full)
            cut = jnp.where(over, i0, cut)
            place = jnp.where(over, 0, used)
            second = jnp.where(over, 1, second)
            visit(a, second, place, low, n)
            return second, place + n, cut

        zero = jnp.int32(0)
        begin = jnp.where(self.shift > 0, agg[W], AD)
        return lax.fori_loop(begin, AD, one, (zero, zero, jnp.int32(-1)))[2]

    def boundary(self, target, limit=RB):
        def one(t, carry):
            a = AD - t
            row = self.agg_start(1, a)
            take = jnp.logical_or(row >= target, carry[0] > limit)
            return jnp.where(take, row, carry[0]), jnp.where(take, a, carry[1])

        row, a = lax.fori_loop(0, AD + 1, one, (jnp.int32(RB), jnp.int32(AD)))
        return jnp.minimum(row, RB), a


def position():
    return lax.axis_index("dom") * lax.axis_size("sub") + lax.axis_index("sub")


def total():
    return lax.axis_size("dom") * lax.axis_size("sub")


def phase_kernel(phase, chunk, halo, *refs):
    refs = list(refs)
    starts, offs, counts, a_hbm, p_hbm = refs[:5]
    del refs[:5]
    if halo:
        before_hbm, after_hbm = refs[:2]
        del refs[:2]
    if phase > 0:
        del refs[0]
    out_hbm = refs.pop(0)
    pack_hbm = refs.pop(0) if chunk is not None else None
    agg, dest, av, pv, acc, blocks = refs[:6]
    row_sems, p_sems, out_sems = refs[6:9]
    if chunk is not None:
        pack, pack_sem = refs[9:11]

    dev = position()
    devices = total()
    frame = Frame(starts, dev, devices)

    p_copies = [pltpu.make_async_copy(p_hbm, pv.at[pl.ds(W, RB)], p_sems.at[0])]
    if halo:
        p_copies.append(pltpu.make_async_copy(before_hbm, pv.at[pl.ds(0, W)], p_sems.at[1]))
        p_copies.append(pltpu.make_async_copy(after_hbm, pv.at[pl.ds(RB + W, W)], p_sems.at[2]))
    for copy in p_copies:
        copy.start()

    frame.fill(agg, RB + 2 * W)

    def remote(a, second, place, low, n):
        dest[a] = jnp.where(second == 1, BASES[1], BASES[0]) + place - low

    cut = frame.chunks(agg, remote)

    def own(a, carry):
        dest[AD + a] = a * KC
        return carry

    lax.fori_loop(0, AD, own, 0)

    own_cut, own_cut_a = frame.boundary(jnp.maximum(frame.shift, FIRST_ROWS))
    r1 = jnp.where(cut >= 0, cut, own_cut)
    r1_a = jnp.where(cut >= 0, 0, own_cut_a)
    e1, e1_a = frame.boundary(jnp.maximum(frame.shift, r1 + FIRST_ROWS), RB - W)
    if phase == 0:
        lo, hi, alo, ahi = r1, e1, r1_a, e1_a
    elif phase == 1:
        lo, hi, alo, ahi = jnp.int32(0), r1, jnp.int32(0), r1_a
    else:
        lo, hi, alo, ahi = e1, jnp.int32(RB), e1_a, jnp.int32(AD)
    rows = hi - lo

    def row_copy(t):
        return pltpu.make_async_copy(a_hbm.at[lo + t], av.at[t], row_sems.at[t])

    def start_row(t, carry):
        row_copy(t).start()
        return carry

    lax.fori_loop(0, rows, start_row, 0)

    def clear(b, carry):
        blocks[b] = jnp.zeros((B, B), F32)
        return carry

    lax.fori_loop(alo * KC, ahi * KC, clear, 0)
    if chunk is not None:
        lax.fori_loop(BASES[chunk], BASES[chunk] + CHUNKS[chunk], clear, 0)
    for copy in p_copies:
        copy.wait()

    j_low = jnp.where(dev == 0, 0, -W)
    j_high = jnp.where(dev == devices - 1, RB, RB + W)

    def group(g, carry):
        places, aggs, firsts, goals = [], [], [], []
        span = jnp.int32(0)
        for u in range(GROUP):
            t = g * GROUP + u

            @pl.when(t < rows)
            def _():
                row_copy(t).wait()

            place = jnp.minimum(t, rows - 1)
            i = lo + place
            a = agg[i + W]
            first = agg[i] - a + W
            span = jnp.maximum(span, agg[i + 2 * W] - a + W - first + 1)
            places.append(place)
            aggs.append(a)
            firsts.append(first)
            goals.append(jnp.where(t < rows, dest[a], -1))

        def compute(slots):
            applied = []
            heads = [jnp.minimum(f, KC - slots) for f in firsts]
            for u in range(GROUP):
                i = lo + places[u]
                for s in range(slots):
                    acc[u, s] = jnp.zeros((B, B), F32)
                used = counts[i]
                for k in range(K):
                    j = i + offs[i, k]
                    ok = jnp.logical_and(k < used, jnp.logical_and(j >= j_low, j < j_high))
                    slot = jnp.where(ok, agg[j + W] - aggs[u] + W - heads[u], KC)
                    product = jnp.dot(
                        av[places[u], k], pv[j + W], preferred_element_type=F32
                    )
                    acc[u, slot] = acc[u, slot] + product
                applied.append(
                    jnp.concatenate([acc[u, s].astype(BF) for s in range(slots)], axis=1)
                )
            for u in range(GROUP):
                i = lo + places[u]
                term = lax.dot_general(
                    pv[i + W], applied[u], (((0,), (0,)), ((), ())), preferred_element_type=F32
                )
                goal = jnp.where(goals[u] >= 0, goals[u] + heads[u], TRASH)
                for s in range(slots):
                    blocks[goal + s] = blocks[goal + s] + term[:, s * B : (s + 1) * B]

        pl.when(span <= 3)(lambda: compute(3))
        pl.when(jnp.logical_and(span > 3, span <= 5))(lambda: compute(5))
        pl.when(span > 5)(lambda: compute(7))
        return carry

    lax.fori_loop(0, lax.div(rows + (GROUP - 1), GROUP), group, 0)

    if chunk is not None:
        size = CHUNKS[chunk]
        for b in range(size):
            pack[b] = blocks[BASES[chunk] + b].astype(BF)
        pack_copy = pltpu.make_async_copy(pack, pack_hbm, pack_sem)
        pack_copy.start()

    def out_copy(a):
        return pltpu.make_async_copy(
            blocks.at[pl.ds(a * KC, KC)], out_hbm.at[a], out_sems.at[a]
        )

    def put(a, carry):
        out_copy(a).start()
        return carry

    def put_wait(a, carry):
        out_copy(a).wait()
        return carry

    lax.fori_loop(alo, ahi, put, 0)
    lax.fori_loop(alo, ahi, put_wait, 0)
    if chunk is not None:
        pack_copy.wait()


def phase_call(phase, chunk, halo, starts, offs, counts, a, p, halos=(), out=None):
    smem = pl.BlockSpec(memory_space=pltpu.SMEM)
    anyspace = pl.BlockSpec(memory_space=pl.ANY)
    operands = [starts, offs, counts, a, p, *halos]
    specs = [smem] * 3 + [anyspace] * (2 + len(halos))
    aliases = {}
    if out is not None:
        aliases = {len(operands): 0}
        operands.append(out)
        specs.append(anyspace)
    shapes = [jax.ShapeDtypeStruct((AD, KC, B, B), F32)]
    scratch = [
        pltpu.SMEM((RB + 2 * W,), jnp.int32),
        pltpu.SMEM((3 * AD,), jnp.int32),
        pltpu.VMEM((RB, K, B, B), BF),
        pltpu.VMEM((RB + 2 * W, B, B), BF),
        pltpu.VMEM((GROUP, K, B, B), F32),
        pltpu.VMEM((BLOCKS, B, B), F32),
        pltpu.SemaphoreType.DMA((RB,)),
        pltpu.SemaphoreType.DMA((3,)),
        pltpu.SemaphoreType.DMA((AD,)),
    ]
    if chunk is not None:
        shapes.append(jax.ShapeDtypeStruct((CHUNKS[chunk], B, B), BF))
        scratch += [pltpu.VMEM((CHUNKS[chunk], B, B), BF), pltpu.SemaphoreType.DMA]
    return pl.pallas_call(
        functools.partial(phase_kernel, phase, chunk, halo),
        out_shape=shapes,
        in_specs=specs,
        out_specs=[anyspace] * len(shapes),
        scratch_shapes=scratch,
        input_output_aliases=aliases,
        compiler_params=pltpu.CompilerParams(vmem_limit_bytes=56 << 20),
        cost_estimate=pl.CostEstimate(
            flops=1_500_000_000, bytes_accessed=8 << 20, transcendentals=0
        ),
        name=f"phase{phase}",
    )(*operands)


def final_kernel(chunk, starts, recv_hbm, out_in, out_hbm, agg, src, dst, recv, blocks, sems, back, recv_sem):
    del out_in
    dev = position()
    devices = total()
    recv_copy = pltpu.make_async_copy(recv_hbm, recv, recv_sem)
    recv_copy.start()
    frame = Frame(starts, dev + 1, devices)
    frame.fill(agg, EDGE)

    def one(a, which, place, low, n):
        @pl.when(which == chunk)
        def _():
            def slot(c, carry):
                src[place + c] = place + c
                dst[place + c] = a * KC + low + c
                return carry

            lax.fori_loop(0, n, slot, 0)
            src[CHUNKS[chunk]] = place + n

    src[CHUNKS[chunk]] = 0
    frame.chunks(agg, one)
    count = src[CHUNKS[chunk]]

    def block(ref, t):
        a = lax.div(dst[t], KC)
        return ref.at[a, dst[t] - a * KC]

    def fetch(t):
        return pltpu.make_async_copy(block(out_hbm, t), blocks.at[t], sems.at[t])

    def store(t):
        return pltpu.make_async_copy(blocks.at[t], block(out_hbm, t), back.at[t])

    def start(t, carry):
        fetch(t).start()
        return carry

    def add(t, carry):
        fetch(t).wait()
        blocks[t] = blocks[t] + recv[t].astype(F32)
        store(t).start()
        return carry

    def finish(t, carry):
        store(t).wait()
        return carry

    lax.fori_loop(0, count, start, 0)
    recv_copy.wait()
    lax.fori_loop(0, count, add, 0)
    lax.fori_loop(0, count, finish, 0)


def final_call(chunk, starts, recv, out):
    smem = pl.BlockSpec(memory_space=pltpu.SMEM)
    anyspace = pl.BlockSpec(memory_space=pl.ANY)
    size = CHUNKS[chunk]
    return pl.pallas_call(
        functools.partial(final_kernel, chunk),
        out_shape=jax.ShapeDtypeStruct((AD, KC, B, B), F32),
        in_specs=[smem, anyspace, anyspace],
        out_specs=anyspace,
        scratch_shapes=[
            pltpu.SMEM((RB + 2 * W,), jnp.int32),
            pltpu.SMEM((size + KC,), jnp.int32),
            pltpu.SMEM((size + KC,), jnp.int32),
            pltpu.VMEM((size, B, B), BF),
            pltpu.VMEM((size, B, B), F32),
            pltpu.SemaphoreType.DMA((size,)),
            pltpu.SemaphoreType.DMA((size,)),
            pltpu.SemaphoreType.DMA,
        ],
        input_output_aliases={2: 0},
        compiler_params=pltpu.CompilerParams(vmem_limit_bytes=24 << 20),
        cost_estimate=pl.CostEstimate(flops=1_000_000, bytes_accessed=4 << 20, transcendentals=0),
        name=f"final{chunk}",
    )(starts, recv, out)


def shards(a_blocks, nbr_offset, nbr_count, prolong, owner_start):
    devices = total()
    axes = ("dom", "sub")
    up = [(i, i + 1) for i in range(devices - 1)]
    down = [(i + 1, i) for i in range(devices - 1)]
    before = lax.ppermute(prolong[RB - W :], axes, up)
    after = lax.ppermute(prolong[:W], axes, down)
    tables = (owner_start, nbr_offset, nbr_count, a_blocks, prolong)
    out, pack_b = phase_call(0, 1, False, *tables)
    recv_b = lax.ppermute(pack_b, axes, down)
    out, pack_a = phase_call(1, 0, True, *tables, halos=(before, after), out=out)
    recv_a = lax.ppermute(pack_a, axes, down)
    (out,) = phase_call(2, None, True, *tables, halos=(before, after), out=out)
    out = final_call(1, owner_start, recv_b, out)
    return final_call(0, owner_start, recv_a, out)


def solution(mesh):
    placed = (
        P(("dom", "sub"), None, None, None),
        P(("dom", "sub"), None),
        P(("dom", "sub")),
        P(("dom", "sub"), None, None),
        P(),
    )
    return jax.shard_map(
        shards,
        mesh=mesh,
        in_specs=placed,
        out_specs=P(("dom", "sub"), None, None, None),
        check_vma=False,
    )
```

```python
import functools

import jax
import jax.numpy as jnp
from jax import lax
from jax.experimental import pallas as pl
from jax.experimental.pallas import tpu as pltpu
from jax.sharding import PartitionSpec as P

BF = jnp.bfloat16
F32 = jnp.float32
W = 3
KC = 7
AD = 16
K = 8
B = 128
RB = 64
CHUNKS = (21, 24)
LAST_ROW = 24
FIRST_ROWS = 20
GROUP = 4
PAD = 7
OWN = AD * KC
SPARE = KC


def bases():
    at, out = OWN + PAD, []
    for size in CHUNKS:
        out.append(at)
        at += size + 2 * PAD
    return out, at


BASES, TRASH = bases()
CLEAR = 8
BLOCKS = -(-(TRASH + KC) // CLEAR) * CLEAR

T_GOAL = K
T_HEAD = K + 1
T_PHASE = K + 2
T_RECV = K + 3
TABLE = (16, 128)
EARLY = 48
VMEM_LIMIT = 8 << 20


class Frame:
    def __init__(self, starts, dev, devices):
        def start_of(d):
            inner = starts[jnp.clip(d, 0, devices - 1)]
            return jnp.where(d >= devices, devices * RB, inner) - dev * RB

        self.initial = dev == 0
        self.final = dev >= devices - 1
        self.begin = [start_of(jnp.maximum(dev - 1, 0)), start_of(dev), start_of(dev + 1)]
        ends = [self.begin[1], self.begin[2], start_of(dev + 2)]
        self.length = [jnp.maximum(e - b, 1) for b, e in zip(self.begin, ends)]
        self.shift = jnp.where(dev >= devices, 0, self.begin[1])
        self.scale = [lax.div(jnp.int32(1 << 20), n) + 1 for n in self.length]

    def agg_start(self, owner, a):
        return self.begin[owner] + lax.shift_right_arithmetic(a * self.length[owner] + (AD - 1), 4)

    def agg(self, i):
        p0, p1, p2 = [i - b for b in self.begin]
        later = jnp.logical_or(p1 >= 0, self.initial)
        last = jnp.logical_and(p2 >= 0, jnp.logical_not(self.final))
        p = jnp.where(last, p2, jnp.where(later, p1, p0))
        m = jnp.where(last, self.scale[2], jnp.where(later, self.scale[1], self.scale[0]))
        o = jnp.where(last, 2 * AD, jnp.where(later, AD, 0))
        a = lax.shift_right_arithmetic(jnp.maximum(p, 0) * AD * m, 20)
        return o + jnp.minimum(a, AD - 1)

    def chunks(self):
        second, used, cut = jnp.int32(0), jnp.int32(0), jnp.int32(-1)
        found = []
        for a in range(AD):
            i0 = jnp.maximum(self.agg_start(0, a), 0)
            i1 = self.agg_start(0, a + 1)
            here = jnp.logical_and(i1 > 0, self.shift > 0)
            low = self.agg(i0 - W) - a + W
            n = jnp.where(here, self.agg(i1 + W - 1) - a + W - low + 1, 0)
            full = jnp.logical_or(used + n > CHUNKS[0], i0 >= LAST_ROW)
            over = jnp.logical_and(jnp.logical_and(second == 0, full), here)
            cut = jnp.where(over, i0, cut)
            place = jnp.where(over, 0, used)
            second = jnp.where(over, 1, second)
            found.append((second, place, low, n))
            used = place + n
        return found, cut

    def boundary(self, target, limit=RB):
        row, before = jnp.int32(RB), jnp.int32(AD)
        for a in range(AD, -1, -1):
            start = self.agg_start(1, a)
            take = jnp.logical_or(start >= target, row > limit)
            row, before = jnp.where(take, start, row), jnp.where(take, a, before)
        return jnp.minimum(row, RB), before


def position():
    return lax.axis_index("dom") * lax.axis_size("sub") + lax.axis_index("sub")


def total():
    return lax.axis_size("dom") * lax.axis_size("sub")


def fill_table(starts, offs, counts, tab):
    dev, devices = position(), total()
    lane = lax.broadcasted_iota(jnp.int32, (1, 128), 1)

    def lanes(values):
        out = jnp.zeros((1, 128), jnp.int32)
        for n, value in enumerate(values):
            out = jnp.where(lane == n, value, out)
        return out

    arriving, _ = Frame(starts, dev + 1, devices).chunks()
    tab[T_RECV : T_RECV + 1] = lanes(
        [((second * 64 + place) * 16 + low) * 16 + n for second, place, low, n in arriving]
    )

    frame = Frame(starts, dev, devices)
    leaving, cut = frame.chunks()

    own_cut, own_cut_a = frame.boundary(jnp.maximum(frame.shift, FIRST_ROWS))
    r1 = jnp.where(cut >= 0, cut, own_cut)
    r1_a = jnp.where(cut >= 0, 0, own_cut_a)
    e1, e1_a = frame.boundary(jnp.maximum(frame.shift, r1 + FIRST_ROWS), EARLY)
    tab[T_PHASE : T_PHASE + 1] = lanes([r1, e1, r1_a, e1_a, 0, r1, 0, r1_a, e1, RB, e1_a, AD])

    i = lane[:, :RB]
    a = frame.agg(i)
    first = frame.agg(i - W) - a + W
    slots = frame.agg(i + W) - a + W - first + 1
    goal = jnp.maximum(a - AD, 0) * KC
    for n, (second, place, low, count) in enumerate(leaving):
        block = jnp.where(second == 1, BASES[1], BASES[0]) + place - low
        goal = jnp.where(a == n, block, goal)
    tab[T_GOAL : T_GOAL + 1, :RB] = goal
    tab[T_HEAD : T_HEAD + 1, :RB] = first + 16 * slots + 256 * jnp.maximum(a - AD, 0)

    j_low = jnp.where(dev == 0, 0, -W)
    j_high = jnp.where(dev == devices - 1, RB, RB + W)
    k = lax.broadcasted_iota(jnp.int32, (K, RB), 0)
    j = lax.broadcasted_iota(jnp.int32, (K, RB), 1) + offs[...]
    ok = jnp.logical_and(k < counts[...], jnp.logical_and(j >= j_low, j < j_high))
    slot = jnp.where(ok, frame.agg(j) - a + W, SPARE)
    tab[:K, :RB] = slot * 256 + j + W


def edges_kernel(
    starts_hbm, offs_hbm, counts_hbm, a_hbm, p_hbm, av, win, blocks, tab,
    starts, offs, counts, send, recv, a_sems, sems,
):
    small = [
        pltpu.make_async_copy(src, dst, sems.at[n])
        for n, (src, dst) in enumerate(
            ((starts_hbm, starts), (offs_hbm, offs), (counts_hbm, counts))
        )
    ]
    parts = a_sems.shape[0]
    size = EARLY // parts
    local = [pltpu.make_async_copy(p_hbm, win.at[pl.ds(W, RB)], sems.at[3])]
    for n in range(parts):
        rows = pl.ds(n * size, size)
        local.append(pltpu.make_async_copy(a_hbm.at[rows], av.at[rows], a_sems.at[n]))

    dev, devices = position(), total()
    cores = lax.axis_size("sub")

    def device(d):
        d = lax.rem(d + devices, devices)
        return (lax.div(d, cores), lax.rem(d, cores))

    left, right = device(dev - 1), device(dev + 1)
    mesh = pl.DeviceIdType.MESH
    barrier = pltpu.get_barrier_semaphore()
    for other in (left, right):
        pl.semaphore_signal(barrier, inc=1, device_id=other, device_id_type=mesh)
    for copy in small + local:
        copy.start()

    for copy in small:
        copy.wait()
    fill_table(starts, offs, counts, tab)

    pl.semaphore_wait(barrier, 2)
    copies = [
        pltpu.make_async_remote_copy(
            src_ref=p_hbm.at[pl.ds(src, W)],
            dst_ref=win.at[pl.ds(dst, W)],
            send_sem=send.at[n],
            recv_sem=recv.at[n],
            device_id=other,
            device_id_type=mesh,
        )
        for n, src, dst, other in ((0, RB - W, 0, right), (1, 0, RB + W, left))
    ]
    for copy in copies:
        copy.start()

    def clear(b, carry):
        for n in range(CLEAR):
            blocks[b * CLEAR + n] = jnp.zeros((B, B), F32)
        return carry

    lax.fori_loop(0, BLOCKS // CLEAR, clear, 0)
    for copy in local + copies:
        copy.wait()


def edges_call(starts, offs, counts, a, p):
    vmem = pl.BlockSpec(memory_space=pltpu.VMEM)
    hbm = pl.BlockSpec(memory_space=pltpu.HBM)
    return pl.pallas_call(
        edges_kernel,
        out_shape=[
            jax.ShapeDtypeStruct((RB, K, B, B), BF),
            jax.ShapeDtypeStruct((RB + 2 * W, B, B), BF),
            jax.ShapeDtypeStruct((BLOCKS, B, B), F32),
            jax.ShapeDtypeStruct(TABLE, jnp.int32),
        ],
        in_specs=[hbm] * 5,
        out_specs=[vmem] * 4,
        scratch_shapes=[
            pltpu.SMEM(starts.shape, jnp.int32),
            pltpu.VMEM(offs.shape, jnp.int32),
            pltpu.VMEM(counts.shape, jnp.int32),
            pltpu.SemaphoreType.DMA((2,)),
            pltpu.SemaphoreType.DMA((2,)),
            pltpu.SemaphoreType.DMA((4,)),
            pltpu.SemaphoreType.DMA((4,)),
        ],
        compiler_params=pltpu.CompilerParams(
            collective_id=0, has_side_effects=True, vmem_limit_bytes=VMEM_LIMIT
        ),
        cost_estimate=pl.CostEstimate(flops=1000, bytes_accessed=20 << 20, transcendentals=0),
        name="edges",
    )(starts, offs, counts, a, p)


def received(tab, a):
    v = tab[T_RECV, a]
    n = jnp.bitwise_and(v, 15)
    low = jnp.bitwise_and(lax.shift_right_logical(v, 4), 15)
    place = jnp.bitwise_and(lax.shift_right_logical(v, 8), 63)
    return lax.shift_right_logical(v, 14), place, low, n


def phase_kernel(phase, *refs):
    refs = list(refs)
    tab_in, win, state, av = refs[:4]
    del refs[:4]
    a_hbm = refs.pop(0) if phase == 0 else None
    arrived = refs.pop(0) if phase == 2 else None
    blocks = refs.pop(0)
    extra = refs.pop(0)
    if phase == 0:
        av = refs.pop(0)
    out_hbm = refs.pop(0) if phase == 2 else None
    tab, acc, tab_sem, out_sems, late_sem = refs
    del state
    late = pl.ds(EARLY, RB - EARLY)
    if phase == 0:
        late_copy = pltpu.make_async_copy(a_hbm.at[late], av.at[late], late_sem)
        late_copy.start()
    chunk = (1, 0, None)[phase]

    tab_copy = pltpu.make_async_copy(tab_in, tab, tab_sem)
    tab_copy.start()
    tab_copy.wait()
    lo, hi, alo, ahi = [tab[T_PHASE, 4 * phase + n] for n in range(4)]
    rows = hi - lo

    def out_copy(a):
        return pltpu.make_async_copy(
            blocks.at[pl.ds(a * KC, KC)], out_hbm.at[a], out_sems.at[a]
        )

    def put(a, carry):
        out_copy(a).start()
        return carry

    def put_wait(a, carry):
        out_copy(a).wait()
        return carry

    if phase == 2:
        lax.fori_loop(0, alo, put, 0)

        def take(a, carry):
            which, place, low, n = received(tab, a)

            def one(s, carry):
                blocks[a * KC + low + s] = arrived[place + s].astype(F32)
                return carry

            lax.fori_loop(0, jnp.where(which == 1, n, 0), one, 0)
            return carry

        lax.fori_loop(alo, ahi, take, 0)

    def group(g, done):
        places, firsts, goals = [], [], []
        span = jnp.int32(0)
        for u in range(GROUP):
            t = g * GROUP + u
            i = lo + jnp.minimum(t, rows - 1)
            head = tab[T_HEAD, i]
            span = jnp.maximum(span, jnp.bitwise_and(lax.shift_right_logical(head, 4), 15))
            places.append(i)
            firsts.append(jnp.bitwise_and(head, 15))
            goals.append(jnp.where(t < rows, tab[T_GOAL, i], TRASH))

        def compute(slots):
            applied = []
            heads = [jnp.minimum(f, KC - slots) for f in firsts]
            for u in range(GROUP):
                i = places[u]
                for s in range(slots):
                    acc[u, heads[u] + s] = jnp.zeros((B, B), F32)
                for k in range(K):
                    code = tab[k, i]
                    slot = lax.shift_right_logical(code, 8)
                    product = jnp.dot(
                        av[i, k],
                        win[jnp.bitwise_and(code, 255)],
                        preferred_element_type=F32,
                    )
                    acc[u, slot] = acc[u, slot] + product
                applied.append(
                    jnp.concatenate(
                        [acc[u, heads[u] + s].astype(BF) for s in range(slots)], axis=1
                    )
                )
            for u in range(GROUP):
                term = lax.dot_general(
                    win[places[u] + W],
                    applied[u],
                    (((0,), (0,)), ((), ())),
                    preferred_element_type=F32,
                )
                goal = goals[u] + heads[u]
                for s in range(slots):
                    blocks[goal + s] = blocks[goal + s] + term[:, s * B : (s + 1) * B]

        pl.when(span <= 3)(lambda: compute(3))
        pl.when(jnp.logical_and(span > 3, span <= 5))(lambda: compute(5))
        pl.when(span > 5)(lambda: compute(7))

        if phase < 2:
            return done
        t = (g + 1) * GROUP
        ahead = lax.shift_right_logical(tab[T_HEAD, lo + jnp.minimum(t, rows - 1)], 8)
        ready = jnp.where(t < rows, jnp.maximum(ahead, alo), alo)
        return lax.fori_loop(done, jnp.maximum(ready, done), lambda a, c: put(a, c + 1), done)

    done = lax.fori_loop(0, lax.div(rows + (GROUP - 1), GROUP), group, alo)
    if chunk is not None:
        for b in range(CHUNKS[chunk]):
            extra[b] = blocks[BASES[chunk] + b].astype(BF)
        if phase == 0:
            late_copy.wait()
        return
    lax.fori_loop(done, ahi, put, 0)
    part = ahi - 1
    for a in range(AD - 1, -1, -1):
        part = jnp.where(received(tab, a)[3] > 0, a, part)
    for c in range(KC):
        extra[c] = blocks[part * KC + c]
    lax.fori_loop(0, ahi, put_wait, 0)


def phase_call(phase, tab, win, blocks, a, more=()):
    vmem = pl.BlockSpec(memory_space=pltpu.VMEM)
    hbm = pl.BlockSpec(memory_space=pltpu.HBM)
    shapes = [jax.ShapeDtypeStruct((BLOCKS, B, B), F32)]
    in_specs = [vmem] * 4
    out_specs = [vmem, vmem]
    aliases = {2: 0}
    if phase == 2:
        shapes.append(jax.ShapeDtypeStruct((KC, B, B), F32))
        shapes.append(jax.ShapeDtypeStruct((AD, KC, B, B), F32))
        in_specs.append(vmem)
        out_specs.append(hbm)
    else:
        shapes.append(jax.ShapeDtypeStruct((CHUNKS[1 - phase], B, B), BF))
    if phase == 0:
        shapes.append(jax.ShapeDtypeStruct((RB, K, B, B), BF))
        in_specs.append(hbm)
        out_specs.append(vmem)
        aliases[3] = 2
    return pl.pallas_call(
        functools.partial(phase_kernel, phase),
        out_shape=shapes,
        in_specs=in_specs,
        out_specs=out_specs,
        scratch_shapes=[
            pltpu.SMEM(TABLE, jnp.int32),
            pltpu.VMEM((GROUP, K, B, B), F32),
            pltpu.SemaphoreType.DMA,
            pltpu.SemaphoreType.DMA((AD,)),
            pltpu.SemaphoreType.DMA,
        ],
        input_output_aliases=aliases,
        compiler_params=pltpu.CompilerParams(vmem_limit_bytes=VMEM_LIMIT),
        cost_estimate=pl.CostEstimate(
            flops=1_500_000_000, bytes_accessed=8 << 20, transcendentals=0
        ),
        name=f"phase{phase}",
    )(tab, win, blocks, a, *more)


def final_kernel(tab_in, arrived, part, out_in, out_hbm, tab, blocks, sems, tab_sem):
    del out_in
    tab_copy = pltpu.make_async_copy(tab_in, tab, tab_sem)
    tab_copy.start()
    tab_copy.wait()

    def store(a, place, low, s):
        at = place + s
        return pltpu.make_async_copy(blocks.at[at], out_hbm.at[a, low + s], sems.at[at])

    def each(act):
        def visit(a, seen):
            which, place, low, n = received(tab, a)
            n = jnp.where(which == 0, n, 0)

            def one(s, carry):
                act(a, place, low, s, seen)
                return carry

            lax.fori_loop(0, n, one, 0)
            return jnp.where(n > 0, 1, seen)

        lax.fori_loop(0, AD, visit, jnp.int32(0))

    def add(a, place, low, s, seen):
        value = arrived[place + s].astype(F32)
        blocks[place + s] = jnp.where(seen == 0, value + part[low + s], value)
        store(a, place, low, s).start()

    each(add)
    each(lambda a, place, low, s, seen: store(a, place, low, s).wait())


def final_call(tab, arrived, part, out):
    vmem = pl.BlockSpec(memory_space=pltpu.VMEM)
    hbm = pl.BlockSpec(memory_space=pltpu.HBM)
    size = CHUNKS[0]
    return pl.pallas_call(
        final_kernel,
        out_shape=jax.ShapeDtypeStruct((AD, KC, B, B), F32),
        in_specs=[vmem, vmem, vmem, hbm],
        out_specs=hbm,
        scratch_shapes=[
            pltpu.SMEM(TABLE, jnp.int32),
            pltpu.VMEM((size, B, B), F32),
            pltpu.SemaphoreType.DMA((size,)),
            pltpu.SemaphoreType.DMA,
        ],
        input_output_aliases={3: 0},
        compiler_params=pltpu.CompilerParams(vmem_limit_bytes=VMEM_LIMIT),
        cost_estimate=pl.CostEstimate(flops=1_000_000, bytes_accessed=4 << 20, transcendentals=0),
        name="final",
    )(tab, arrived, part, out)


def shards(a_blocks, nbr_offset, nbr_count, prolong, owner_start):
    axes = ("dom", "sub")
    down = [(i + 1, i) for i in range(total() - 1)]
    inputs = (owner_start, nbr_offset.T, nbr_count.reshape(1, RB), a_blocks, prolong)
    inputs = [pltpu.with_memory_space_constraint(x, pltpu.HBM) for x in inputs]
    a, win, blocks, tab = edges_call(*inputs)
    blocks, pack_b, a = phase_call(0, tab, win, blocks, a, inputs[3:4])
    recv_b = lax.ppermute(pack_b, axes, down)
    blocks, pack_a = phase_call(1, tab, win, blocks, a)
    recv_a = lax.ppermute(pack_a, axes, down)
    blocks, part, out = phase_call(2, tab, win, blocks, a, (recv_b,))
    return final_call(tab, recv_a, part, out)


def solution(mesh):
    placed = (
        P(("dom", "sub"), None, None, None),
        P(("dom", "sub"), None),
        P(("dom", "sub")),
        P(("dom", "sub"), None, None),
        P(),
    )
    return jax.shard_map(
        shards,
        mesh=mesh,
        in_specs=placed,
        out_specs=P(("dom", "sub"), None, None, None),
        check_vma=False,
    )
```

```python
import functools

import jax
import jax.numpy as jnp
from jax import lax
from jax.experimental import pallas as pl
from jax.experimental.pallas import tpu as pltpu
from jax.sharding import PartitionSpec as P

BF = jnp.bfloat16
F32 = jnp.float32
W = 3
KC = 7
AD = 16
K = 8
B = 128
RB = 64
CHUNKS = (21, 24)
LAST_ROW = 28
FIRST_ROWS = 16
SECOND_ROWS = 26
GROUP = 4
PAD = 7
OWN = AD * KC
SPARE = KC


def bases():
    at, out = OWN + PAD, []
    for size in CHUNKS:
        out.append(at)
        at += size + 2 * PAD
    return out, at


BASES, TRASH = bases()
CLEAR = 8
BLOCKS = -(-(TRASH + KC) // CLEAR) * CLEAR

T_GOAL = K
T_HEAD = K + 1
T_PHASE = K + 2
T_RECV = K + 3
TABLE = (16, 128)
EARLY = 32
PIECE = 4
VMEM_LIMIT = 8 << 20


class Frame:
    def __init__(self, starts, dev, devices):
        def start_of(d):
            inner = starts[jnp.clip(d, 0, devices - 1)]
            return jnp.where(d >= devices, devices * RB, inner) - dev * RB

        self.initial = dev == 0
        self.final = dev >= devices - 1
        self.begin = [start_of(jnp.maximum(dev - 1, 0)), start_of(dev), start_of(dev + 1)]
        ends = [self.begin[1], self.begin[2], start_of(dev + 2)]
        self.length = [jnp.maximum(e - b, 1) for b, e in zip(self.begin, ends)]
        self.shift = jnp.where(dev >= devices, 0, self.begin[1])
        self.scale = [lax.div(jnp.int32(1 << 20), n) + 1 for n in self.length]

    def agg_start(self, owner, a):
        return self.begin[owner] + lax.shift_right_arithmetic(a * self.length[owner] + (AD - 1), 4)

    def agg(self, i):
        p0, p1, p2 = [i - b for b in self.begin]
        later = jnp.logical_or(p1 >= 0, self.initial)
        last = jnp.logical_and(p2 >= 0, jnp.logical_not(self.final))
        p = jnp.where(last, p2, jnp.where(later, p1, p0))
        m = jnp.where(last, self.scale[2], jnp.where(later, self.scale[1], self.scale[0]))
        o = jnp.where(last, 2 * AD, jnp.where(later, AD, 0))
        a = lax.shift_right_arithmetic(jnp.maximum(p, 0) * AD * m, 20)
        return o + jnp.minimum(a, AD - 1)

    def chunks(self):
        second, used, cut = jnp.int32(0), jnp.int32(0), jnp.int32(-1)
        found = []
        for a in range(AD):
            i0 = jnp.maximum(self.agg_start(0, a), 0)
            i1 = self.agg_start(0, a + 1)
            here = jnp.logical_and(i1 > 0, self.shift > 0)
            low = self.agg(i0 - W) - a + W
            n = jnp.where(here, self.agg(i1 + W - 1) - a + W - low + 1, 0)
            full = jnp.logical_or(used + n > CHUNKS[0], i0 >= LAST_ROW)
            over = jnp.logical_and(jnp.logical_and(second == 0, full), here)
            cut = jnp.where(over, i0, cut)
            place = jnp.where(over, 0, used)
            second = jnp.where(over, 1, second)
            found.append((second, place, low, n))
            used = place + n
        return found, cut

    def boundary(self, target, limit=RB):
        row, before = jnp.int32(RB), jnp.int32(AD)
        for a in range(AD, -1, -1):
            start = self.agg_start(1, a)
            take = jnp.logical_or(start >= target, row > limit)
            row, before = jnp.where(take, start, row), jnp.where(take, a, before)
        return jnp.minimum(row, RB), before


def position():
    return lax.axis_index("dom") * lax.axis_size("sub") + lax.axis_index("sub")


def total():
    return lax.axis_size("dom") * lax.axis_size("sub")


def fill_table(starts, offs, counts, tab):
    dev, devices = position(), total()
    lane = lax.broadcasted_iota(jnp.int32, (1, 128), 1)

    def lanes(values):
        out = jnp.zeros((1, 128), jnp.int32)
        for n, value in enumerate(values):
            out = jnp.where(lane == n, value, out)
        return out

    arriving, _ = Frame(starts, dev + 1, devices).chunks()
    tab[T_RECV : T_RECV + 1] = lanes(
        [((second * 64 + place) * 16 + low) * 16 + n for second, place, low, n in arriving]
    )

    frame = Frame(starts, dev, devices)
    leaving, cut = frame.chunks()

    own_cut, _ = frame.boundary(jnp.maximum(frame.shift, FIRST_ROWS))
    r1 = jnp.where(cut >= 0, cut, own_cut)
    e1, _ = frame.boundary(jnp.maximum(frame.shift, r1 + FIRST_ROWS), RB - W)
    e2, e2_a = frame.boundary(e1 + jnp.maximum(SECOND_ROWS - r1, 0), RB - W)
    tab[T_PHASE : T_PHASE + 1] = lanes([r1, e1, e2, e2_a])

    i = lane[:, :RB]
    a = frame.agg(i)
    first = frame.agg(i - W) - a + W
    slots = frame.agg(i + W) - a + W - first + 1
    goal = jnp.maximum(a - AD, 0) * KC
    for n, (second, place, low, count) in enumerate(leaving):
        block = jnp.where(second == 1, BASES[1], BASES[0]) + place - low
        goal = jnp.where(a == n, block, goal)
    tab[T_GOAL : T_GOAL + 1, :RB] = goal
    tab[T_HEAD : T_HEAD + 1, :RB] = first + 16 * slots + 256 * jnp.maximum(a - AD, 0)

    j_low = jnp.where(dev == 0, 0, -W)
    j_high = jnp.where(dev == devices - 1, RB, RB + W)
    k = lax.broadcasted_iota(jnp.int32, (K, RB), 0)
    j = lax.broadcasted_iota(jnp.int32, (K, RB), 1) + offs[...]
    ok = jnp.logical_and(k < counts[...], jnp.logical_and(j >= j_low, j < j_high))
    slot = jnp.where(ok, frame.agg(j) - a + W, SPARE)
    tab[:K, :RB] = slot * 256 + j + W


def edges_kernel(
    starts_hbm, offs_hbm, counts_hbm, a_hbm, p_hbm, av, win, blocks, tab,
    starts, offs, counts, send, recv, a_sems, sems,
):
    small = [
        pltpu.make_async_copy(src, dst, sems.at[n])
        for n, (src, dst) in enumerate(
            ((starts_hbm, starts), (offs_hbm, offs), (counts_hbm, counts))
        )
    ]
    parts = a_sems.shape[0]
    size = EARLY // parts
    local = [pltpu.make_async_copy(p_hbm, win.at[pl.ds(W, RB)], sems.at[3])]
    for n in range(parts):
        rows = pl.ds(n * size, size)
        local.append(pltpu.make_async_copy(a_hbm.at[rows], av.at[rows], a_sems.at[n]))

    dev, devices = position(), total()
    cores = lax.axis_size("sub")
    mesh = pl.DeviceIdType.MESH

    def device(d):
        return (lax.div(d, cores), lax.rem(d, cores))

    left, right = device(jnp.maximum(dev - 1, 0)), device(jnp.minimum(dev + 1, devices - 1))
    has_left, has_right = dev > 0, dev < devices - 1
    sides = ((has_left, left), (has_right, right))
    barrier = pltpu.get_barrier_semaphore()
    for has, other in sides:

        @pl.when(has)
        def _(other=other):
            pl.semaphore_signal(barrier, inc=1, device_id=other, device_id_type=mesh)

    for copy in small + local:
        copy.start()

    for copy in small:
        copy.wait()
    fill_table(starts, offs, counts, tab)

    neighbours = has_left.astype(jnp.int32) + has_right.astype(jnp.int32)
    pl.semaphore_wait(barrier, neighbours)
    copies = [
        pltpu.make_async_remote_copy(
            src_ref=p_hbm.at[pl.ds(src, W)],
            dst_ref=win.at[pl.ds(dst, W)],
            send_sem=send.at[n],
            recv_sem=recv.at[n],
            device_id=other,
            device_id_type=mesh,
        )
        for n, src, dst, other in ((0, 0, RB + W, left), (1, RB - W, 0, right))
    ]
    for (has, _), copy in zip(sides, copies):
        pl.when(has)(copy.start)

    def clear(b, carry):
        for n in range(CLEAR):
            blocks[b * CLEAR + n] = jnp.zeros((B, B), F32)
        return carry

    lax.fori_loop(0, BLOCKS // CLEAR, clear, 0)
    for copy in local:
        copy.wait()
    for (has, _), copy, at, arrival in zip(sides, copies, (0, RB + W), copies[::-1]):
        pl.when(has)(copy.wait_send)
        pl.when(has)(arrival.wait_recv)

        @pl.when(jnp.logical_not(has))
        def _(at=at):
            for n in range(W):
                win[at + n] = jnp.zeros((B, B), BF)


def edges_call(starts, offs, counts, a, p):
    vmem = pl.BlockSpec(memory_space=pltpu.VMEM)
    hbm = pl.BlockSpec(memory_space=pltpu.HBM)
    return pl.pallas_call(
        edges_kernel,
        out_shape=[
            jax.ShapeDtypeStruct((RB, K, B, B), BF),
            jax.ShapeDtypeStruct((RB + 2 * W, B, B), BF),
            jax.ShapeDtypeStruct((BLOCKS, B, B), F32),
            jax.ShapeDtypeStruct(TABLE, jnp.int32),
        ],
        in_specs=[hbm] * 5,
        out_specs=[vmem] * 4,
        scratch_shapes=[
            pltpu.SMEM(starts.shape, jnp.int32),
            pltpu.VMEM(offs.shape, jnp.int32),
            pltpu.VMEM(counts.shape, jnp.int32),
            pltpu.SemaphoreType.DMA((2,)),
            pltpu.SemaphoreType.DMA((2,)),
            pltpu.SemaphoreType.DMA((4,)),
            pltpu.SemaphoreType.DMA((4,)),
        ],
        compiler_params=pltpu.CompilerParams(
            collective_id=0, has_side_effects=True, vmem_limit_bytes=VMEM_LIMIT
        ),
        cost_estimate=pl.CostEstimate(flops=1000, bytes_accessed=20 << 20, transcendentals=0),
        name="edges",
    )(starts, offs, counts, a, p)


def received(tab, a):
    v = tab[T_RECV, a]
    n = jnp.bitwise_and(v, 15)
    low = jnp.bitwise_and(lax.shift_right_logical(v, 4), 15)
    place = jnp.bitwise_and(lax.shift_right_logical(v, 8), 63)
    return lax.shift_right_logical(v, 14), place, low, n


def phase_kernel(phase, *refs):
    refs = list(refs)
    tab_in, win, state, av = refs[:4]
    del refs[:4]
    a_hbm = refs.pop(0) if phase == 0 else None
    blocks = refs.pop(0)
    extra = refs.pop(0)
    if phase == 0:
        av = refs.pop(0)
    out_hbm = refs.pop(0) if phase == 2 else None
    tab, *acc, tab_sem, out_sems, late_sems = refs
    del state

    def late_copy(n):
        rows = pl.ds(EARLY + n * PIECE, PIECE)
        return pltpu.make_async_copy(a_hbm.at[rows], av.at[rows], late_sems.at[n])

    def late_wait(n, carry):
        late_copy(n).wait()
        return carry

    late = (RB - EARLY) // PIECE
    if phase == 0:
        for n in range(late):
            late_copy(n).start()
    chunk = (1, 0, None)[phase]

    tab_copy = pltpu.make_async_copy(tab_in, tab, tab_sem)
    tab_copy.start()
    tab_copy.wait()
    r1, e1, e2, e2_a = [tab[T_PHASE, n] for n in range(4)]
    rows = (e1 - r1, r1 + e2 - e1, RB - e2)[phase]

    def row_at(t):
        if phase == 1:
            return t + jnp.where(t < r1, 0, e1 - r1)
        return t + (r1, 0, e2)[phase]

    def out_copy(a):
        return pltpu.make_async_copy(
            blocks.at[pl.ds(a * KC, KC)], out_hbm.at[a], out_sems.at[a]
        )

    def put(a, carry):
        out_copy(a).start()
        return carry

    def put_wait(a, carry):
        out_copy(a).wait()
        return carry

    if phase == 2:
        lax.fori_loop(0, e2_a, put, 0)

    def group(g, done):
        if phase == 0:
            last = row_at(jnp.minimum(g * GROUP + GROUP, rows))
            need = lax.div(jnp.maximum(last - EARLY, 0) + (PIECE - 1), PIECE)
            done = lax.fori_loop(done, need, lambda n, c: late_wait(n, c + 1), done)
        places, firsts, goals = [], [], []
        span = jnp.int32(0)
        for u in range(GROUP):
            t = g * GROUP + u
            i = row_at(jnp.minimum(t, rows - 1))
            head = tab[T_HEAD, i]
            span = jnp.maximum(span, jnp.bitwise_and(lax.shift_right_logical(head, 4), 15))
            places.append(i)
            firsts.append(jnp.bitwise_and(head, 15))
            goals.append(jnp.where(t < rows, tab[T_GOAL, i], TRASH))

        def compute(slots):
            applied = []
            heads = [jnp.minimum(f, KC - slots) for f in firsts]
            for u in range(GROUP):
                for s in range(slots):
                    acc[u][heads[u] + s] = jnp.zeros((B, B), F32)
            for k in range(K):
                for u in range(GROUP):
                    i = places[u]
                    code = tab[k, i]
                    slot = lax.shift_right_logical(code, 8)
                    product = jnp.dot(
                        av[i, k],
                        win[jnp.bitwise_and(code, 255)],
                        preferred_element_type=F32,
                    )
                    acc[u][slot] = acc[u][slot] + product
            for u in range(GROUP):
                applied.append(
                    jnp.concatenate(
                        [acc[u][heads[u] + s].astype(BF) for s in range(slots)], axis=1
                    )
                )
            for u in range(GROUP):
                term = lax.dot_general(
                    win[places[u] + W],
                    applied[u],
                    (((0,), (0,)), ((), ())),
                    preferred_element_type=F32,
                )
                goal = goals[u] + heads[u]
                for s in range(slots):
                    blocks[goal + s] = blocks[goal + s] + term[:, s * B : (s + 1) * B]

        pl.when(span <= 3)(lambda: compute(3))
        pl.when(jnp.logical_and(span > 3, span <= 5))(lambda: compute(5))
        pl.when(span > 5)(lambda: compute(7))

        if phase < 2:
            return done
        t = (g + 1) * GROUP
        ahead = lax.shift_right_logical(tab[T_HEAD, row_at(jnp.minimum(t, rows - 1))], 8)
        ready = jnp.where(t < rows, ahead, done)
        return lax.fori_loop(done, jnp.maximum(ready, done), lambda a, c: put(a, c + 1), done)

    start = (0, 0, e2_a)[phase]
    done = lax.fori_loop(0, lax.div(rows + (GROUP - 1), GROUP), group, jnp.int32(start))
    if chunk is not None:
        for b in range(CHUNKS[chunk]):
            extra[b] = blocks[BASES[chunk] + b].astype(BF)
        if phase == 0:
            lax.fori_loop(done, late, late_wait, 0)
        return
    lax.fori_loop(done, AD, put, 0)
    part = jnp.int32(AD - 1)
    for a in range(AD - 1, -1, -1):
        part = jnp.where(received(tab, a)[3] > 0, a, part)
    for c in range(KC):
        extra[c] = blocks[part * KC + c]
    lax.fori_loop(0, AD, put_wait, 0)


def phase_call(phase, tab, win, blocks, a, more=()):
    vmem = pl.BlockSpec(memory_space=pltpu.VMEM)
    hbm = pl.BlockSpec(memory_space=pltpu.HBM)
    shapes = [jax.ShapeDtypeStruct((BLOCKS, B, B), F32)]
    in_specs = [vmem] * 4
    out_specs = [vmem, vmem]
    aliases = {2: 0}
    if phase == 2:
        shapes.append(jax.ShapeDtypeStruct((KC, B, B), F32))
        shapes.append(jax.ShapeDtypeStruct((AD, KC, B, B), F32))
        out_specs.append(hbm)
    else:
        shapes.append(jax.ShapeDtypeStruct((CHUNKS[1 - phase], B, B), BF))
    if phase == 0:
        shapes.append(jax.ShapeDtypeStruct((RB, K, B, B), BF))
        in_specs.append(hbm)
        out_specs.append(vmem)
        aliases[3] = 2
    return pl.pallas_call(
        functools.partial(phase_kernel, phase),
        out_shape=shapes,
        in_specs=in_specs,
        out_specs=out_specs,
        scratch_shapes=[
            pltpu.SMEM(TABLE, jnp.int32),
            *[pltpu.VMEM((K, B, B), F32)] * GROUP,
            pltpu.SemaphoreType.DMA,
            pltpu.SemaphoreType.DMA((AD,)),
            pltpu.SemaphoreType.DMA(((RB - EARLY) // PIECE,)),
        ],
        input_output_aliases=aliases,
        compiler_params=pltpu.CompilerParams(vmem_limit_bytes=VMEM_LIMIT),
        cost_estimate=pl.CostEstimate(
            flops=1_500_000_000, bytes_accessed=8 << 20, transcendentals=0
        ),
        name=f"phase{phase}",
    )(tab, win, blocks, a, *more)


def final_kernel(tab_in, first, second, part, out_in, out_hbm, tab, blocks, sems, tab_sem):
    del out_in
    tab_copy = pltpu.make_async_copy(tab_in, tab, tab_sem)
    tab_copy.start()
    tab_copy.wait()

    def store(a, at, slot):
        return pltpu.make_async_copy(blocks.at[at], out_hbm.at[a, slot], sems.at[at])

    def each(act):
        def visit(a, seen):
            which, place, low, n = received(tab, a)

            def one(s, carry):
                act(a, which, place + s, low + s, seen)
                return carry

            lax.fori_loop(0, n, one, 0)
            return jnp.where(n > 0, 1, seen)

        lax.fori_loop(0, AD, visit, jnp.int32(0))

    def add(a, which, place, slot, seen):
        @pl.when(seen == 0)
        def _():
            blocks[place] = first[place].astype(F32) + part[slot]

        @pl.when(jnp.logical_and(seen > 0, which == 0))
        def _():
            blocks[place] = first[place].astype(F32)

        @pl.when(which == 1)
        def _():
            blocks[CHUNKS[0] + place] = second[place].astype(F32)

        store(a, which * CHUNKS[0] + place, slot).start()

    each(add)
    each(lambda a, which, place, slot, seen: store(a, which * CHUNKS[0] + place, slot).wait())


def final_call(tab, first, second, part, out):
    vmem = pl.BlockSpec(memory_space=pltpu.VMEM)
    hbm = pl.BlockSpec(memory_space=pltpu.HBM)
    size = sum(CHUNKS)
    return pl.pallas_call(
        final_kernel,
        out_shape=jax.ShapeDtypeStruct((AD, KC, B, B), F32),
        in_specs=[vmem, vmem, vmem, vmem, hbm],
        out_specs=hbm,
        scratch_shapes=[
            pltpu.SMEM(TABLE, jnp.int32),
            pltpu.VMEM((size, B, B), F32),
            pltpu.SemaphoreType.DMA((size,)),
            pltpu.SemaphoreType.DMA,
        ],
        input_output_aliases={4: 0},
        compiler_params=pltpu.CompilerParams(vmem_limit_bytes=VMEM_LIMIT),
        cost_estimate=pl.CostEstimate(flops=1_000_000, bytes_accessed=4 << 20, transcendentals=0),
        name="final",
    )(tab, first, second, part, out)


def shards(a_blocks, nbr_offset, nbr_count, prolong, owner_start):
    axes = ("dom", "sub")
    down = [(i + 1, i) for i in range(total() - 1)]
    inputs = (owner_start, nbr_offset.T, nbr_count.reshape(1, RB), a_blocks, prolong)
    inputs = [pltpu.with_memory_space_constraint(x, pltpu.HBM) for x in inputs]
    a, win, blocks, tab = edges_call(*inputs)
    blocks, pack_b, a = phase_call(0, tab, win, blocks, a, inputs[3:4])
    recv_b = lax.ppermute(pack_b, axes, down)
    blocks, pack_a = phase_call(1, tab, win, blocks, a)
    recv_a = lax.ppermute(pack_a, axes, down)
    blocks, part, out = phase_call(2, tab, win, blocks, a)
    return final_call(tab, recv_a, recv_b, part, out)


def solution(mesh):
    placed = (
        P(("dom", "sub"), None, None, None),
        P(("dom", "sub"), None),
        P(("dom", "sub")),
        P(("dom", "sub"), None, None),
        P(),
    )
    return jax.shard_map(
        shards,
        mesh=mesh,
        in_specs=placed,
        out_specs=P(("dom", "sub"), None, None, None),
        check_vma=False,
    )
```

```python
import functools

import jax
import jax.numpy as jnp
from jax import lax
from jax.experimental import pallas as pl
from jax.experimental.pallas import tpu as pltpu
from jax.sharding import PartitionSpec as P

BF = jnp.bfloat16
F32 = jnp.float32
W = 3
KC = 7
AD = 16
K = 8
B = 128
RB = 64
CHUNKS = (21, 24)
LAST_ROW = 28
FIRST_ROWS = 12
SECOND_ROWS = 26
GROUP = 4
PAD = 7
OWN = AD * KC
SPARE = KC


def bases():
    at, out = OWN + PAD, []
    for size in CHUNKS:
        out.append(at)
        at += size + 2 * PAD
    return out, at


BASES, TRASH = bases()
CLEAR = 8
BLOCKS = -(-(TRASH + KC) // CLEAR) * CLEAR

T_GOAL = K
T_HEAD = K + 1
T_PHASE = K + 2
T_RECV = K + 3
TABLE = (16, 128)
EARLY = 32
PIECE = 4
VMEM_LIMIT = 8 << 20


class Frame:
    def __init__(self, starts, dev, devices):
        def start_of(d):
            inner = starts[jnp.clip(d, 0, devices - 1)]
            return jnp.where(d >= devices, devices * RB, inner) - dev * RB

        self.initial = dev == 0
        self.final = dev >= devices - 1
        self.begin = [start_of(jnp.maximum(dev - 1, 0)), start_of(dev), start_of(dev + 1)]
        ends = [self.begin[1], self.begin[2], start_of(dev + 2)]
        self.length = [jnp.maximum(e - b, 1) for b, e in zip(self.begin, ends)]
        self.shift = jnp.where(dev >= devices, 0, self.begin[1])
        self.scale = [lax.div(jnp.int32(1 << 20), n) + 1 for n in self.length]

    def agg_start(self, owner, a):
        return self.begin[owner] + lax.shift_right_arithmetic(a * self.length[owner] + (AD - 1), 4)

    def agg(self, i):
        p0, p1, p2 = [i - b for b in self.begin]
        later = jnp.logical_or(p1 >= 0, self.initial)
        last = jnp.logical_and(p2 >= 0, jnp.logical_not(self.final))
        p = jnp.where(last, p2, jnp.where(later, p1, p0))
        m = jnp.where(last, self.scale[2], jnp.where(later, self.scale[1], self.scale[0]))
        o = jnp.where(last, 2 * AD, jnp.where(later, AD, 0))
        a = lax.shift_right_arithmetic(jnp.maximum(p, 0) * AD * m, 20)
        return o + jnp.minimum(a, AD - 1)

    def chunks(self):
        second, used, cut = jnp.int32(0), jnp.int32(0), jnp.int32(-1)
        found = []
        for a in range(AD):
            i0 = jnp.maximum(self.agg_start(0, a), 0)
            i1 = self.agg_start(0, a + 1)
            here = jnp.logical_and(i1 > 0, self.shift > 0)
            low = self.agg(i0 - W) - a + W
            n = jnp.where(here, self.agg(i1 + W - 1) - a + W - low + 1, 0)
            full = jnp.logical_or(used + n > CHUNKS[0], i0 >= LAST_ROW)
            over = jnp.logical_and(jnp.logical_and(second == 0, full), here)
            cut = jnp.where(over, i0, cut)
            place = jnp.where(over, 0, used)
            second = jnp.where(over, 1, second)
            found.append((second, place, low, n))
            used = place + n
        return found, cut

    def boundary(self, target, limit=RB):
        row, before = jnp.int32(RB), jnp.int32(AD)
        for a in range(AD, -1, -1):
            start = self.agg_start(1, a)
            take = jnp.logical_or(start >= target, row > limit)
            row, before = jnp.where(take, start, row), jnp.where(take, a, before)
        return jnp.minimum(row, RB), before


def position():
    return lax.axis_index("dom") * lax.axis_size("sub") + lax.axis_index("sub")


def total():
    return lax.axis_size("dom") * lax.axis_size("sub")


def fill_table(starts, offs, counts, tab):
    dev, devices = position(), total()
    lane = lax.broadcasted_iota(jnp.int32, (1, 128), 1)

    def lanes(values):
        out = jnp.zeros((1, 128), jnp.int32)
        for n, value in enumerate(values):
            out = jnp.where(lane == n, value, out)
        return out

    arriving, _ = Frame(starts, dev + 1, devices).chunks()
    tab[T_RECV : T_RECV + 1] = lanes(
        [((second * 64 + place) * 16 + low) * 16 + n for second, place, low, n in arriving]
    )

    frame = Frame(starts, dev, devices)
    leaving, cut = frame.chunks()

    own_cut, _ = frame.boundary(jnp.maximum(frame.shift, FIRST_ROWS))
    r1 = jnp.where(cut >= 0, cut, own_cut)
    e1, _ = frame.boundary(jnp.maximum(frame.shift, r1 + FIRST_ROWS), RB - W)
    e2, e2_a = frame.boundary(e1 + jnp.maximum(SECOND_ROWS - r1, 0), RB - W)
    tab[T_PHASE : T_PHASE + 1] = lanes([r1, e1, e2, e2_a])

    i = lane[:, :RB]
    a = frame.agg(i)
    first = frame.agg(i - W) - a + W
    slots = frame.agg(i + W) - a + W - first + 1
    goal = jnp.maximum(a - AD, 0) * KC
    for n, (second, place, low, count) in enumerate(leaving):
        block = jnp.where(second == 1, BASES[1], BASES[0]) + place - low
        goal = jnp.where(a == n, block, goal)
    tab[T_GOAL : T_GOAL + 1, :RB] = goal
    tab[T_HEAD : T_HEAD + 1, :RB] = first + 16 * slots + 256 * jnp.maximum(a - AD, 0)

    j_low = jnp.where(dev == 0, 0, -W)
    j_high = jnp.where(dev == devices - 1, RB, RB + W)
    k = lax.broadcasted_iota(jnp.int32, (K, RB), 0)
    j = lax.broadcasted_iota(jnp.int32, (K, RB), 1) + offs[...]
    ok = jnp.logical_and(k < counts[...], jnp.logical_and(j >= j_low, j < j_high))
    slot = jnp.where(ok, frame.agg(j) - a + W, SPARE)
    tab[:K, :RB] = slot * 256 + j + W


def edges_kernel(
    starts_hbm, offs_hbm, counts_hbm, a_hbm, p_hbm, av, win, blocks, tab,
    starts, offs, counts, send, recv, a_sems, sems,
):
    small = [
        pltpu.make_async_copy(src, dst, sems.at[n])
        for n, (src, dst) in enumerate(
            ((starts_hbm, starts), (offs_hbm, offs), (counts_hbm, counts))
        )
    ]
    parts = a_sems.shape[0]
    size = EARLY // parts
    local = [pltpu.make_async_copy(p_hbm, win.at[pl.ds(W, RB)], sems.at[3])]
    for n in range(parts):
        rows = pl.ds(n * size, size)
        local.append(pltpu.make_async_copy(a_hbm.at[rows], av.at[rows], a_sems.at[n]))

    dev, devices = position(), total()
    cores = lax.axis_size("sub")
    mesh = pl.DeviceIdType.MESH

    def device(d):
        return (lax.div(d, cores), lax.rem(d, cores))

    left, right = device(jnp.maximum(dev - 1, 0)), device(jnp.minimum(dev + 1, devices - 1))
    has_left, has_right = dev > 0, dev < devices - 1
    sides = ((has_left, left), (has_right, right))
    barrier = pltpu.get_barrier_semaphore()
    for has, other in sides:

        @pl.when(has)
        def _(other=other):
            pl.semaphore_signal(barrier, inc=1, device_id=other, device_id_type=mesh)

    for copy in small + local:
        copy.start()

    neighbours = has_left.astype(jnp.int32) + has_right.astype(jnp.int32)
    pl.semaphore_wait(barrier, neighbours)
    copies = [
        pltpu.make_async_remote_copy(
            src_ref=p_hbm.at[pl.ds(src, W)],
            dst_ref=win.at[pl.ds(dst, W)],
            send_sem=send.at[n],
            recv_sem=recv.at[n],
            device_id=other,
            device_id_type=mesh,
        )
        for n, src, dst, other in ((0, 0, RB + W, left), (1, RB - W, 0, right))
    ]
    for (has, _), copy in zip(sides, copies):
        pl.when(has)(copy.start)

    def clear(b, carry):
        for n in range(CLEAR):
            blocks[b * CLEAR + n] = jnp.zeros((B, B), F32)
        return carry

    lax.fori_loop(0, BLOCKS // CLEAR, clear, 0)
    for copy in small:
        copy.wait()
    fill_table(starts, offs, counts, tab)
    for copy in local:
        copy.wait()
    for (has, _), copy, at, arrival in zip(sides, copies, (0, RB + W), copies[::-1]):
        pl.when(has)(copy.wait_send)
        pl.when(has)(arrival.wait_recv)

        @pl.when(jnp.logical_not(has))
        def _(at=at):
            for n in range(W):
                win[at + n] = jnp.zeros((B, B), BF)


def edges_call(starts, offs, counts, a, p):
    vmem = pl.BlockSpec(memory_space=pltpu.VMEM)
    hbm = pl.BlockSpec(memory_space=pltpu.HBM)
    return pl.pallas_call(
        edges_kernel,
        out_shape=[
            jax.ShapeDtypeStruct((RB, K, B, B), BF),
            jax.ShapeDtypeStruct((RB + 2 * W, B, B), BF),
            jax.ShapeDtypeStruct((BLOCKS, B, B), F32),
            jax.ShapeDtypeStruct(TABLE, jnp.int32),
        ],
        in_specs=[hbm] * 5,
        out_specs=[vmem] * 4,
        scratch_shapes=[
            pltpu.SMEM(starts.shape, jnp.int32),
            pltpu.VMEM(offs.shape, jnp.int32),
            pltpu.VMEM(counts.shape, jnp.int32),
            pltpu.SemaphoreType.DMA((2,)),
            pltpu.SemaphoreType.DMA((2,)),
            pltpu.SemaphoreType.DMA((4,)),
            pltpu.SemaphoreType.DMA((4,)),
        ],
        compiler_params=pltpu.CompilerParams(
            collective_id=0, has_side_effects=True, vmem_limit_bytes=VMEM_LIMIT
        ),
        cost_estimate=pl.CostEstimate(flops=1000, bytes_accessed=20 << 20, transcendentals=0),
        name="edges",
    )(starts, offs, counts, a, p)


def received(tab, a):
    v = tab[T_RECV, a]
    n = jnp.bitwise_and(v, 15)
    low = jnp.bitwise_and(lax.shift_right_logical(v, 4), 15)
    place = jnp.bitwise_and(lax.shift_right_logical(v, 8), 63)
    return lax.shift_right_logical(v, 14), place, low, n


def phase_kernel(phase, *refs):
    refs = list(refs)
    tab_in, win, state, av = refs[:4]
    del refs[:4]
    a_hbm = refs.pop(0) if phase == 0 else None
    arrived = refs.pop(0) if phase == 2 else None
    blocks = refs.pop(0)
    extra = refs.pop(0)
    if phase == 0:
        av = refs.pop(0)
    out_hbm = refs.pop(0) if phase == 2 else None
    tab, *acc, tab_sem, out_sems, late_sems = refs
    del state

    def late_copy(n):
        rows = pl.ds(EARLY + n * PIECE, PIECE)
        return pltpu.make_async_copy(a_hbm.at[rows], av.at[rows], late_sems.at[n])

    def late_wait(n, carry):
        late_copy(n).wait()
        return carry

    late = (RB - EARLY) // PIECE
    if phase == 0:
        for n in range(late):
            late_copy(n).start()
    chunk = (1, 0, None)[phase]

    tab_copy = pltpu.make_async_copy(tab_in, tab, tab_sem)
    tab_copy.start()
    tab_copy.wait()
    r1, e1, e2, e2_a = [tab[T_PHASE, n] for n in range(4)]
    rows = (e1 - r1, r1 + e2 - e1, RB - e2)[phase]

    def row_at(t):
        if phase == 1:
            return t + jnp.where(t < r1, 0, e1 - r1)
        return t + (r1, 0, e2)[phase]

    def out_copy(a):
        return pltpu.make_async_copy(
            blocks.at[pl.ds(a * KC, KC)], out_hbm.at[a], out_sems.at[a]
        )

    def put(a, carry):
        out_copy(a).start()
        return carry

    def put_wait(a, carry):
        out_copy(a).wait()
        return carry

    if phase == 2:
        lax.fori_loop(0, e2_a, put, 0)

        def take(a, carry):
            which, place, low, n = received(tab, a)

            def one(s, carry):
                blocks[a * KC + low + s] = arrived[place + s].astype(F32)
                return carry

            lax.fori_loop(0, jnp.where(which == 1, n, 0), one, 0)
            return carry

        lax.fori_loop(e2_a, AD, take, 0)

    def group(g, done):
        if phase == 0:
            last = row_at(jnp.minimum(g * GROUP + GROUP, rows))
            need = lax.div(jnp.maximum(last - EARLY, 0) + (PIECE - 1), PIECE)
            done = lax.fori_loop(done, need, lambda n, c: late_wait(n, c + 1), done)
        places, firsts, goals = [], [], []
        span = jnp.int32(0)
        for u in range(GROUP):
            t = g * GROUP + u
            i = row_at(jnp.minimum(t, rows - 1))
            head = tab[T_HEAD, i]
            span = jnp.maximum(span, jnp.bitwise_and(lax.shift_right_logical(head, 4), 15))
            places.append(i)
            firsts.append(jnp.bitwise_and(head, 15))
            goals.append(jnp.where(t < rows, tab[T_GOAL, i], TRASH))

        def compute(slots):
            applied = []
            heads = [jnp.minimum(f, KC - slots) for f in firsts]
            for u in range(GROUP):
                for s in range(slots):
                    acc[u][heads[u] + s] = jnp.zeros((B, B), F32)
            for k in range(K):
                for u in range(GROUP):
                    i = places[u]
                    code = tab[k, i]
                    slot = lax.shift_right_logical(code, 8)
                    product = jnp.dot(
                        av[i, k],
                        win[jnp.bitwise_and(code, 255)],
                        preferred_element_type=F32,
                    )
                    acc[u][slot] = acc[u][slot] + product
            for u in range(GROUP):
                applied.append(
                    jnp.concatenate(
                        [acc[u][heads[u] + s].astype(BF) for s in range(slots)], axis=1
                    )
                )
            for u in range(GROUP):
                term = lax.dot_general(
                    win[places[u] + W],
                    applied[u],
                    (((0,), (0,)), ((), ())),
                    preferred_element_type=F32,
                )
                goal = goals[u] + heads[u]
                for s in range(slots):
                    blocks[goal + s] = blocks[goal + s] + term[:, s * B : (s + 1) * B]

        pl.when(span <= 3)(lambda: compute(3))
        pl.when(jnp.logical_and(span > 3, span <= 5))(lambda: compute(5))
        pl.when(span > 5)(lambda: compute(7))

        if phase < 2:
            return done
        t = (g + 1) * GROUP
        ahead = lax.shift_right_logical(tab[T_HEAD, row_at(jnp.minimum(t, rows - 1))], 8)
        ready = jnp.where(t < rows, ahead, done)
        return lax.fori_loop(done, jnp.maximum(ready, done), lambda a, c: put(a, c + 1), done)

    start = (0, 0, e2_a)[phase]
    done = lax.fori_loop(0, lax.div(rows + (GROUP - 1), GROUP), group, jnp.int32(start))
    if chunk is not None:
        for b in range(CHUNKS[chunk]):
            extra[b] = blocks[BASES[chunk] + b].astype(BF)
        if phase == 0:
            lax.fori_loop(done, late, late_wait, 0)
        return
    lax.fori_loop(done, AD, put, 0)
    part = jnp.int32(AD - 1)
    for a in range(AD - 1, -1, -1):
        part = jnp.where(received(tab, a)[3] > 0, a, part)
    for c in range(KC):
        extra[c] = blocks[part * KC + c]
    lax.fori_loop(0, AD, put_wait, 0)


def phase_call(phase, tab, win, blocks, a, more=()):
    vmem = pl.BlockSpec(memory_space=pltpu.VMEM)
    hbm = pl.BlockSpec(memory_space=pltpu.HBM)
    shapes = [jax.ShapeDtypeStruct((BLOCKS, B, B), F32)]
    in_specs = [vmem] * 4
    out_specs = [vmem, vmem]
    aliases = {2: 0}
    if phase == 2:
        shapes.append(jax.ShapeDtypeStruct((KC, B, B), F32))
        shapes.append(jax.ShapeDtypeStruct((AD, KC, B, B), F32))
        in_specs.append(vmem)
        out_specs.append(hbm)
    else:
        shapes.append(jax.ShapeDtypeStruct((CHUNKS[1 - phase], B, B), BF))
    if phase == 0:
        shapes.append(jax.ShapeDtypeStruct((RB, K, B, B), BF))
        in_specs.append(hbm)
        out_specs.append(vmem)
        aliases[3] = 2
    return pl.pallas_call(
        functools.partial(phase_kernel, phase),
        out_shape=shapes,
        in_specs=in_specs,
        out_specs=out_specs,
        scratch_shapes=[
            pltpu.SMEM(TABLE, jnp.int32),
            *[pltpu.VMEM((K, B, B), F32)] * GROUP,
            pltpu.SemaphoreType.DMA,
            pltpu.SemaphoreType.DMA((AD,)),
            pltpu.SemaphoreType.DMA(((RB - EARLY) // PIECE,)),
        ],
        input_output_aliases=aliases,
        compiler_params=pltpu.CompilerParams(vmem_limit_bytes=VMEM_LIMIT),
        cost_estimate=pl.CostEstimate(
            flops=1_500_000_000, bytes_accessed=8 << 20, transcendentals=0
        ),
        name=f"phase{phase}",
    )(tab, win, blocks, a, *more)


def final_kernel(tab_in, arrived, part, out_in, out_hbm, tab, blocks, sems, tab_sem):
    del out_in
    tab_copy = pltpu.make_async_copy(tab_in, tab, tab_sem)
    tab_copy.start()
    tab_copy.wait()

    def store(a, place, slot):
        return pltpu.make_async_copy(blocks.at[place], out_hbm.at[a, slot], sems.at[place])

    def each(act):
        def visit(a, seen):
            which, place, low, n = received(tab, a)

            def one(s, carry):
                act(a, place + s, low + s, seen)
                return carry

            lax.fori_loop(0, jnp.where(which == 0, n, 0), one, 0)
            return jnp.where(n > 0, 1, seen)

        lax.fori_loop(0, AD, visit, jnp.int32(0))

    def add(a, place, slot, seen):
        value = arrived[place].astype(F32)
        blocks[place] = jnp.where(seen == 0, value + part[slot], value)
        store(a, place, slot).start()

    each(add)
    each(lambda a, place, slot, seen: store(a, place, slot).wait())


def final_call(tab, arrived, part, out):
    vmem = pl.BlockSpec(memory_space=pltpu.VMEM)
    hbm = pl.BlockSpec(memory_space=pltpu.HBM)
    size = CHUNKS[0]
    return pl.pallas_call(
        final_kernel,
        out_shape=jax.ShapeDtypeStruct((AD, KC, B, B), F32),
        in_specs=[vmem, vmem, vmem, hbm],
        out_specs=hbm,
        scratch_shapes=[
            pltpu.SMEM(TABLE, jnp.int32),
            pltpu.VMEM((size, B, B), F32),
            pltpu.SemaphoreType.DMA((size,)),
            pltpu.SemaphoreType.DMA,
        ],
        input_output_aliases={3: 0},
        compiler_params=pltpu.CompilerParams(vmem_limit_bytes=VMEM_LIMIT),
        cost_estimate=pl.CostEstimate(flops=1_000_000, bytes_accessed=4 << 20, transcendentals=0),
        name="final",
    )(tab, arrived, part, out)


def shards(a_blocks, nbr_offset, nbr_count, prolong, owner_start):
    axes = ("dom", "sub")
    down = [(i + 1, i) for i in range(total() - 1)]
    inputs = (owner_start, nbr_offset.T, nbr_count.reshape(1, RB), a_blocks, prolong)
    inputs = [pltpu.with_memory_space_constraint(x, pltpu.HBM) for x in inputs]
    a, win, blocks, tab = edges_call(*inputs)
    blocks, pack_b, a = phase_call(0, tab, win, blocks, a, inputs[3:4])
    recv_b = lax.ppermute(pack_b, axes, down)
    blocks, pack_a = phase_call(1, tab, win, blocks, a)
    recv_a = lax.ppermute(pack_a, axes, down)
    blocks, part, out = phase_call(2, tab, win, blocks, a, (recv_b,))
    return final_call(tab, recv_a, part, out)


def solution(mesh):
    placed = (
        P(("dom", "sub"), None, None, None),
        P(("dom", "sub"), None),
        P(("dom", "sub")),
        P(("dom", "sub"), None, None),
        P(),
    )
    return jax.shard_map(
        shards,
        mesh=mesh,
        in_specs=placed,
        out_specs=P(("dom", "sub"), None, None, None),
        check_vma=False,
    )
```

```python
import functools

import jax
import jax.numpy as jnp
from jax import lax
from jax.experimental import pallas as pl
from jax.experimental.pallas import tpu as pltpu
from jax.sharding import PartitionSpec as P

BF = jnp.bfloat16
F32 = jnp.float32
W = 3
KC = 7
AD = 16
K = 8
B = 128
RB = 64
CHUNKS = (21, 24)
LAST_ROW = 28
FIRST_ROWS = 12
SECOND_ROWS = 26
GROUP = 4
PAD = 7
OWN = AD * KC
SPARE = KC


def bases():
    at, out = OWN + PAD, []
    for size in CHUNKS:
        out.append(at)
        at += size + 2 * PAD
    return out, at


BASES, TRASH = bases()
CLEAR = 8
BLOCKS = -(-(TRASH + KC) // CLEAR) * CLEAR

T_GOAL = K
T_HEAD = K + 1
T_PHASE = K + 2
T_RECV = K + 3
TABLE = (16, 128)
EARLY = 32
PIECE = 4
VMEM_LIMIT = 8 << 20


class Frame:
    def __init__(self, starts, dev, devices):
        def start_of(d):
            inner = starts[jnp.clip(d, 0, devices - 1)]
            return jnp.where(d >= devices, devices * RB, inner) - dev * RB

        self.initial = dev == 0
        self.final = dev >= devices - 1
        self.begin = [start_of(jnp.maximum(dev - 1, 0)), start_of(dev), start_of(dev + 1)]
        ends = [self.begin[1], self.begin[2], start_of(dev + 2)]
        self.length = [jnp.maximum(e - b, 1) for b, e in zip(self.begin, ends)]
        self.shift = jnp.where(dev >= devices, 0, self.begin[1])
        self.scale = [lax.div(jnp.int32(1 << 20), n) + 1 for n in self.length]

    def agg_start(self, owner, a):
        return self.begin[owner] + lax.shift_right_arithmetic(a * self.length[owner] + (AD - 1), 4)

    def agg(self, i):
        p0, p1, p2 = [i - b for b in self.begin]
        later = jnp.logical_or(p1 >= 0, self.initial)
        last = jnp.logical_and(p2 >= 0, jnp.logical_not(self.final))
        p = jnp.where(last, p2, jnp.where(later, p1, p0))
        m = jnp.where(last, self.scale[2], jnp.where(later, self.scale[1], self.scale[0]))
        o = jnp.where(last, 2 * AD, jnp.where(later, AD, 0))
        a = lax.shift_right_arithmetic(jnp.maximum(p, 0) * AD * m, 20)
        return o + jnp.minimum(a, AD - 1)

    def chunks(self):
        second, used, cut = jnp.int32(0), jnp.int32(0), jnp.int32(-1)
        found = []
        for a in range(AD):
            i0 = jnp.maximum(self.agg_start(0, a), 0)
            i1 = self.agg_start(0, a + 1)
            here = jnp.logical_and(i1 > 0, self.shift > 0)
            low = self.agg(i0 - W) - a + W
            n = jnp.where(here, self.agg(i1 + W - 1) - a + W - low + 1, 0)
            full = jnp.logical_or(used + n > CHUNKS[0], i0 >= LAST_ROW)
            over = jnp.logical_and(jnp.logical_and(second == 0, full), here)
            cut = jnp.where(over, i0, cut)
            place = jnp.where(over, 0, used)
            second = jnp.where(over, 1, second)
            found.append((second, place, low, n))
            used = place + n
        return found, cut

    def boundary(self, target, limit=RB):
        row, before = jnp.int32(RB), jnp.int32(AD)
        for a in range(AD, -1, -1):
            start = self.agg_start(1, a)
            take = jnp.logical_or(start >= target, row > limit)
            row, before = jnp.where(take, start, row), jnp.where(take, a, before)
        return jnp.minimum(row, RB), before


def position():
    return lax.axis_index("dom") * lax.axis_size("sub") + lax.axis_index("sub")


def total():
    return lax.axis_size("dom") * lax.axis_size("sub")


def fill_table(starts, offs, counts, tab):
    dev, devices = position(), total()
    lane = lax.broadcasted_iota(jnp.int32, (1, 128), 1)

    def lanes(values):
        out = jnp.zeros((1, 128), jnp.int32)
        for n, value in enumerate(values):
            out = jnp.where(lane == n, value, out)
        return out

    arriving, _ = Frame(starts, dev + 1, devices).chunks()
    tab[T_RECV : T_RECV + 1] = lanes(
        [((second * 64 + place) * 16 + low) * 16 + n for second, place, low, n in arriving]
    )

    frame = Frame(starts, dev, devices)
    leaving, cut = frame.chunks()

    own_cut, _ = frame.boundary(jnp.maximum(frame.shift, FIRST_ROWS))
    r1 = jnp.where(cut >= 0, cut, own_cut)
    e1, _ = frame.boundary(jnp.maximum(frame.shift, r1 + FIRST_ROWS), RB - W)
    e2, e2_a = frame.boundary(e1 + jnp.maximum(SECOND_ROWS - r1, 0), RB - W)
    tab[T_PHASE : T_PHASE + 1] = lanes([r1, e1, e2, e2_a])

    i = lane[:, :RB]
    a = frame.agg(i)
    first = frame.agg(i - W) - a + W
    slots = frame.agg(i + W) - a + W - first + 1
    goal = jnp.maximum(a - AD, 0) * KC
    for n, (second, place, low, count) in enumerate(leaving):
        block = jnp.where(second == 1, BASES[1], BASES[0]) + place - low
        goal = jnp.where(a == n, block, goal)
    tab[T_GOAL : T_GOAL + 1, :RB] = goal
    tab[T_HEAD : T_HEAD + 1, :RB] = first + 16 * slots + 256 * jnp.maximum(a - AD, 0)

    j_low = jnp.where(dev == 0, 0, -W)
    j_high = jnp.where(dev == devices - 1, RB, RB + W)
    k = lax.broadcasted_iota(jnp.int32, (K, RB), 0)
    j = lax.broadcasted_iota(jnp.int32, (K, RB), 1) + offs[...]
    ok = jnp.logical_and(k < counts[...], jnp.logical_and(j >= j_low, j < j_high))
    slot = jnp.where(ok, frame.agg(j) - a + W, SPARE)
    tab[:K, :RB] = slot * 256 + j + W


def edges_kernel(
    starts_hbm, offs_hbm, counts_hbm, a_hbm, p_hbm, av, win, blocks, tab,
    starts, offs, counts, send, recv, a_sems, sems,
):
    small = [
        pltpu.make_async_copy(src, dst, sems.at[n])
        for n, (src, dst) in enumerate(
            ((starts_hbm, starts), (offs_hbm, offs), (counts_hbm, counts))
        )
    ]
    parts = a_sems.shape[0]
    size = EARLY // parts
    local = [pltpu.make_async_copy(p_hbm, win.at[pl.ds(W, RB)], sems.at[3])]
    for n in range(parts):
        rows = pl.ds(n * size, size)
        local.append(pltpu.make_async_copy(a_hbm.at[rows], av.at[rows], a_sems.at[n]))

    dev, devices = position(), total()
    cores = lax.axis_size("sub")
    mesh = pl.DeviceIdType.MESH

    def device(d):
        return (lax.div(d, cores), lax.rem(d, cores))

    left, right = device(jnp.maximum(dev - 1, 0)), device(jnp.minimum(dev + 1, devices - 1))
    has_left, has_right = dev > 0, dev < devices - 1
    sides = ((has_left, left), (has_right, right))
    barrier = pltpu.get_barrier_semaphore()
    for has, other in sides:

        @pl.when(has)
        def _(other=other):
            pl.semaphore_signal(barrier, inc=1, device_id=other, device_id_type=mesh)

    for copy in small + local:
        copy.start()

    neighbours = has_left.astype(jnp.int32) + has_right.astype(jnp.int32)
    pl.semaphore_wait(barrier, neighbours)
    copies = [
        pltpu.make_async_remote_copy(
            src_ref=p_hbm.at[pl.ds(src, W)],
            dst_ref=win.at[pl.ds(dst, W)],
            send_sem=send.at[n],
            recv_sem=recv.at[n],
            device_id=other,
            device_id_type=mesh,
        )
        for n, src, dst, other in ((0, 0, RB + W, left), (1, RB - W, 0, right))
    ]
    for (has, _), copy in zip(sides, copies):
        pl.when(has)(copy.start)

    def clear(b, carry):
        for n in range(CLEAR):
            blocks[b * CLEAR + n] = jnp.zeros((B, B), F32)
        return carry

    lax.fori_loop(0, BLOCKS // CLEAR, clear, 0)
    for copy in small:
        copy.wait()
    fill_table(starts, offs, counts, tab)
    for copy in local:
        copy.wait()
    for (has, _), copy, at, arrival in zip(sides, copies, (0, RB + W), copies[::-1]):
        pl.when(has)(copy.wait_send)
        pl.when(has)(arrival.wait_recv)

        @pl.when(jnp.logical_not(has))
        def _(at=at):
            for n in range(W):
                win[at + n] = jnp.zeros((B, B), BF)


def edges_call(starts, offs, counts, a, p):
    vmem = pl.BlockSpec(memory_space=pltpu.VMEM)
    hbm = pl.BlockSpec(memory_space=pltpu.HBM)
    return pl.pallas_call(
        edges_kernel,
        out_shape=[
            jax.ShapeDtypeStruct((RB, K, B, B), BF),
            jax.ShapeDtypeStruct((RB + 2 * W, B, B), BF),
            jax.ShapeDtypeStruct((BLOCKS, B, B), F32),
            jax.ShapeDtypeStruct(TABLE, jnp.int32),
        ],
        in_specs=[hbm] * 5,
        out_specs=[vmem] * 4,
        scratch_shapes=[
            pltpu.SMEM(starts.shape, jnp.int32),
            pltpu.VMEM(offs.shape, jnp.int32),
            pltpu.VMEM(counts.shape, jnp.int32),
            pltpu.SemaphoreType.DMA((2,)),
            pltpu.SemaphoreType.DMA((2,)),
            pltpu.SemaphoreType.DMA((4,)),
            pltpu.SemaphoreType.DMA((4,)),
        ],
        compiler_params=pltpu.CompilerParams(
            collective_id=0, has_side_effects=True, vmem_limit_bytes=VMEM_LIMIT
        ),
        cost_estimate=pl.CostEstimate(flops=1000, bytes_accessed=20 << 20, transcendentals=0),
        name="edges",
    )(starts, offs, counts, a, p)


def received(tab, a):
    v = tab[T_RECV, a]
    n = jnp.bitwise_and(v, 15)
    low = jnp.bitwise_and(lax.shift_right_logical(v, 4), 15)
    place = jnp.bitwise_and(lax.shift_right_logical(v, 8), 63)
    return lax.shift_right_logical(v, 14), place, low, n


def phase_kernel(phase, *refs):
    refs = list(refs)
    tab_in, win, state, av = refs[:4]
    del refs[:4]
    a_hbm = refs.pop(0) if phase == 0 else None
    arrived = refs.pop(0) if phase == 2 else None
    blocks = refs.pop(0)
    extra = refs.pop(0)
    if phase == 0:
        av = refs.pop(0)
    out_hbm = refs.pop(0) if phase == 2 else None
    tab, *acc, tab_sem, out_sems, late_sems = refs
    del state

    def late_copy(n):
        rows = pl.ds(EARLY + n * PIECE, PIECE)
        return pltpu.make_async_copy(a_hbm.at[rows], av.at[rows], late_sems.at[n])

    def late_wait(n, carry):
        late_copy(n).wait()
        return carry

    late = (RB - EARLY) // PIECE
    if phase == 0:
        for n in range(late):
            late_copy(n).start()
    chunk = (1, 0, None)[phase]

    tab_copy = pltpu.make_async_copy(tab_in, tab, tab_sem)
    tab_copy.start()
    tab_copy.wait()
    r1, e1, e2, e2_a = [tab[T_PHASE, n] for n in range(4)]
    rows = (e1 - r1, r1 + e2 - e1, RB - e2)[phase]

    def row_at(t):
        if phase == 1:
            return t + jnp.where(t < r1, 0, e1 - r1)
        return t + (r1, 0, e2)[phase]

    def out_copy(a):
        return pltpu.make_async_copy(
            blocks.at[pl.ds(a * KC, KC)], out_hbm.at[a], out_sems.at[a]
        )

    def put(a, carry):
        out_copy(a).start()
        return carry

    def put_wait(a, carry):
        out_copy(a).wait()
        return carry

    if phase == 2:
        lax.fori_loop(0, e2_a, put, 0)

        def take(a, carry):
            which, place, low, n = received(tab, a)

            def one(s, carry):
                blocks[a * KC + low + s] = arrived[place + s].astype(F32)
                return carry

            lax.fori_loop(0, jnp.where(which == 1, n, 0), one, 0)
            return carry

        lax.fori_loop(e2_a, AD, take, 0)

        part = jnp.int32(AD - 1)
        for a in range(AD - 1, -1, -1):
            part = jnp.where(received(tab, a)[3] > 0, a, part)
        lax.fori_loop(part + 1, AD, put, 0)

    def group(g, done):
        if phase == 0:
            last = row_at(jnp.minimum(g * GROUP + GROUP, rows))
            need = lax.div(jnp.maximum(last - EARLY, 0) + (PIECE - 1), PIECE)
            done = lax.fori_loop(done, need, lambda n, c: late_wait(n, c + 1), done)
        places, firsts, goals = [], [], []
        span = jnp.int32(0)
        for u in range(GROUP):
            t = g * GROUP + u
            i = row_at(jnp.minimum(t, rows - 1))
            head = tab[T_HEAD, i]
            span = jnp.maximum(span, jnp.bitwise_and(lax.shift_right_logical(head, 4), 15))
            places.append(i)
            firsts.append(jnp.bitwise_and(head, 15))
            goals.append(jnp.where(t < rows, tab[T_GOAL, i], TRASH))

        def compute(slots):
            applied = []
            heads = [jnp.minimum(f, KC - slots) for f in firsts]
            for u in range(GROUP):
                for s in range(slots):
                    acc[u][heads[u] + s] = jnp.zeros((B, B), F32)
            for k in range(K):
                for u in range(GROUP):
                    i = places[u]
                    code = tab[k, i]
                    slot = lax.shift_right_logical(code, 8)
                    product = jnp.dot(
                        av[i, k],
                        win[jnp.bitwise_and(code, 255)],
                        preferred_element_type=F32,
                    )
                    acc[u][slot] = acc[u][slot] + product
            for u in range(GROUP):
                applied.append(
                    jnp.concatenate(
                        [acc[u][heads[u] + s].astype(BF) for s in range(slots)], axis=1
                    )
                )
            for u in range(GROUP):
                term = lax.dot_general(
                    win[places[u] + W],
                    applied[u],
                    (((0,), (0,)), ((), ())),
                    preferred_element_type=F32,
                )
                goal = goals[u] + heads[u]
                for s in range(slots):
                    blocks[goal + s] = blocks[goal + s] + term[:, s * B : (s + 1) * B]

        pl.when(span <= 3)(lambda: compute(3))
        pl.when(jnp.logical_and(span > 3, span <= 5))(lambda: compute(5))
        pl.when(span > 5)(lambda: compute(7))

        if phase < 2:
            return done
        t = (g + 1) * GROUP
        ahead = lax.shift_right_logical(tab[T_HEAD, row_at(jnp.minimum(t, rows - 1))], 8)
        ready = jnp.where(t < rows, ahead, done)
        return lax.fori_loop(done, jnp.maximum(ready, done), lambda a, c: put(a, c + 1), done)

    start = (0, 0, e2_a)[phase]
    done = lax.fori_loop(0, lax.div(rows + (GROUP - 1), GROUP), group, jnp.int32(start))
    if chunk is not None:
        for b in range(CHUNKS[chunk]):
            extra[b] = blocks[BASES[chunk] + b].astype(BF)
        if phase == 0:
            lax.fori_loop(done, late, late_wait, 0)
        return
    lax.fori_loop(done, part + 1, put, 0)
    for c in range(KC):
        extra[c] = blocks[part * KC + c]
    lax.fori_loop(0, AD, put_wait, 0)


def phase_call(phase, tab, win, blocks, a, more=()):
    vmem = pl.BlockSpec(memory_space=pltpu.VMEM)
    hbm = pl.BlockSpec(memory_space=pltpu.HBM)
    shapes = [jax.ShapeDtypeStruct((BLOCKS, B, B), F32)]
    in_specs = [vmem] * 4
    out_specs = [vmem, vmem]
    aliases = {2: 0}
    if phase == 2:
        shapes.append(jax.ShapeDtypeStruct((KC, B, B), F32))
        shapes.append(jax.ShapeDtypeStruct((AD, KC, B, B), F32))
        in_specs.append(vmem)
        out_specs.append(hbm)
    else:
        shapes.append(jax.ShapeDtypeStruct((CHUNKS[1 - phase], B, B), BF))
    if phase == 0:
        shapes.append(jax.ShapeDtypeStruct((RB, K, B, B), BF))
        in_specs.append(hbm)
        out_specs.append(vmem)
        aliases[3] = 2
    return pl.pallas_call(
        functools.partial(phase_kernel, phase),
        out_shape=shapes,
        in_specs=in_specs,
        out_specs=out_specs,
        scratch_shapes=[
            pltpu.SMEM(TABLE, jnp.int32),
            *[pltpu.VMEM((K, B, B), F32)] * GROUP,
            pltpu.SemaphoreType.DMA,
            pltpu.SemaphoreType.DMA((AD,)),
            pltpu.SemaphoreType.DMA(((RB - EARLY) // PIECE,)),
        ],
        input_output_aliases=aliases,
        compiler_params=pltpu.CompilerParams(vmem_limit_bytes=VMEM_LIMIT),
        cost_estimate=pl.CostEstimate(
            flops=1_500_000_000, bytes_accessed=8 << 20, transcendentals=0
        ),
        name=f"phase{phase}",
    )(tab, win, blocks, a, *more)


def final_kernel(tab_in, arrived, part, out_in, out_hbm, tab, blocks, sems, tab_sem):
    del out_in
    tab_copy = pltpu.make_async_copy(tab_in, tab, tab_sem)
    tab_copy.start()
    tab_copy.wait()

    def store(a, place, slot):
        return pltpu.make_async_copy(blocks.at[place], out_hbm.at[a, slot], sems.at[place])

    def each(act):
        def visit(a, seen):
            which, place, low, n = received(tab, a)

            def one(s, carry):
                act(a, place + s, low + s, seen)
                return carry

            lax.fori_loop(0, jnp.where(which == 0, n, 0), one, 0)
            return jnp.where(n > 0, 1, seen)

        lax.fori_loop(0, AD, visit, jnp.int32(0))

    def add(a, place, slot, seen):
        value = arrived[place].astype(F32)
        blocks[place] = jnp.where(seen == 0, value + part[slot], value)
        store(a, place, slot).start()

    each(add)
    each(lambda a, place, slot, seen: store(a, place, slot).wait())


def final_call(tab, arrived, part, out):
    vmem = pl.BlockSpec(memory_space=pltpu.VMEM)
    hbm = pl.BlockSpec(memory_space=pltpu.HBM)
    size = CHUNKS[0]
    return pl.pallas_call(
        final_kernel,
        out_shape=jax.ShapeDtypeStruct((AD, KC, B, B), F32),
        in_specs=[vmem, vmem, vmem, hbm],
        out_specs=hbm,
        scratch_shapes=[
            pltpu.SMEM(TABLE, jnp.int32),
            pltpu.VMEM((size, B, B), F32),
            pltpu.SemaphoreType.DMA((size,)),
            pltpu.SemaphoreType.DMA,
        ],
        input_output_aliases={3: 0},
        compiler_params=pltpu.CompilerParams(vmem_limit_bytes=VMEM_LIMIT),
        cost_estimate=pl.CostEstimate(flops=1_000_000, bytes_accessed=4 << 20, transcendentals=0),
        name="final",
    )(tab, arrived, part, out)


def shards(a_blocks, nbr_offset, nbr_count, prolong, owner_start):
    axes = ("dom", "sub")
    down = [(i + 1, i) for i in range(total() - 1)]
    inputs = (owner_start, nbr_offset.T, nbr_count.reshape(1, RB), a_blocks, prolong)
    inputs = [pltpu.with_memory_space_constraint(x, pltpu.HBM) for x in inputs]
    a, win, blocks, tab = edges_call(*inputs)
    blocks, pack_b, a = phase_call(0, tab, win, blocks, a, inputs[3:4])
    recv_b = lax.ppermute(pack_b, axes, down)
    blocks, pack_a = phase_call(1, tab, win, blocks, a)
    recv_a = lax.ppermute(pack_a, axes, down)
    blocks, part, out = phase_call(2, tab, win, blocks, a, (recv_b,))
    return final_call(tab, recv_a, part, out)


def solution(mesh):
    placed = (
        P(("dom", "sub"), None, None, None),
        P(("dom", "sub"), None),
        P(("dom", "sub")),
        P(("dom", "sub"), None, None),
        P(),
    )
    return jax.shard_map(
        shards,
        mesh=mesh,
        in_specs=placed,
        out_specs=P(("dom", "sub"), None, None, None),
        check_vma=False,
    )
```

```python
import functools

import jax
import jax.numpy as jnp
from jax import lax
from jax.experimental import pallas as pl
from jax.experimental.pallas import tpu as pltpu
from jax.sharding import PartitionSpec as P

BF = jnp.bfloat16
F32 = jnp.float32
W = 3
KC = 7
AD = 16
K = 8
B = 128
RB = 64
CHUNKS = (21, 24)
LAST_ROW = 28
FIRST_ROWS = 8
SECOND_ROWS = 30
GROUP = 4
PAD = 7
OWN = AD * KC
SPARE = KC


def bases():
    at, out = OWN + PAD, []
    for size in CHUNKS:
        out.append(at)
        at += size + 2 * PAD
    return out, at


BASES, TRASH = bases()
CLEAR = 8
BLOCKS = -(-(TRASH + KC) // CLEAR) * CLEAR

T_GOAL = K
T_HEAD = K + 1
T_PHASE = K + 2
T_RECV = K + 3
TABLE = (16, 128)
EARLY = 32
PIECE = 4
VMEM_LIMIT = 8 << 20


class Frame:
    def __init__(self, starts, dev, devices):
        def start_of(d):
            inner = starts[jnp.clip(d, 0, devices - 1)]
            return jnp.where(d >= devices, devices * RB, inner) - dev * RB

        self.initial = dev == 0
        self.final = dev >= devices - 1
        self.begin = [start_of(jnp.maximum(dev - 1, 0)), start_of(dev), start_of(dev + 1)]
        ends = [self.begin[1], self.begin[2], start_of(dev + 2)]
        self.length = [jnp.maximum(e - b, 1) for b, e in zip(self.begin, ends)]
        self.shift = jnp.where(dev >= devices, 0, self.begin[1])
        self.scale = [lax.div(jnp.int32(1 << 20), n) + 1 for n in self.length]

    def agg_start(self, owner, a):
        return self.begin[owner] + lax.shift_right_arithmetic(a * self.length[owner] + (AD - 1), 4)

    def agg(self, i):
        p0, p1, p2 = [i - b for b in self.begin]
        later = jnp.logical_or(p1 >= 0, self.initial)
        last = jnp.logical_and(p2 >= 0, jnp.logical_not(self.final))
        p = jnp.where(last, p2, jnp.where(later, p1, p0))
        m = jnp.where(last, self.scale[2], jnp.where(later, self.scale[1], self.scale[0]))
        o = jnp.where(last, 2 * AD, jnp.where(later, AD, 0))
        a = lax.shift_right_arithmetic(jnp.maximum(p, 0) * AD * m, 20)
        return o + jnp.minimum(a, AD - 1)

    def chunks(self):
        second, used, cut = jnp.int32(0), jnp.int32(0), jnp.int32(-1)
        found = []
        for a in range(AD):
            i0 = jnp.maximum(self.agg_start(0, a), 0)
            i1 = self.agg_start(0, a + 1)
            here = jnp.logical_and(i1 > 0, self.shift > 0)
            low = self.agg(i0 - W) - a + W
            n = jnp.where(here, self.agg(i1 + W - 1) - a + W - low + 1, 0)
            full = jnp.logical_or(used + n > CHUNKS[0], i0 >= LAST_ROW)
            over = jnp.logical_and(jnp.logical_and(second == 0, full), here)
            cut = jnp.where(over, i0, cut)
            place = jnp.where(over, 0, used)
            second = jnp.where(over, 1, second)
            found.append((second, place, low, n))
            used = place + n
        return found, cut

    def boundary(self, target, limit=RB):
        row, before = jnp.int32(RB), jnp.int32(AD)
        for a in range(AD, -1, -1):
            start = self.agg_start(1, a)
            take = jnp.logical_or(start >= target, row > limit)
            row, before = jnp.where(take, start, row), jnp.where(take, a, before)
        return jnp.minimum(row, RB), before


def position():
    return lax.axis_index("dom") * lax.axis_size("sub") + lax.axis_index("sub")


def total():
    return lax.axis_size("dom") * lax.axis_size("sub")


def fill_table(starts, offs, counts, tab):
    dev, devices = position(), total()
    lane = lax.broadcasted_iota(jnp.int32, (1, 128), 1)

    def lanes(values):
        out = jnp.zeros((1, 128), jnp.int32)
        for n, value in enumerate(values):
            out = jnp.where(lane == n, value, out)
        return out

    arriving, _ = Frame(starts, dev + 1, devices).chunks()
    tab[T_RECV : T_RECV + 1] = lanes(
        [((second * 64 + place) * 16 + low) * 16 + n for second, place, low, n in arriving]
    )

    frame = Frame(starts, dev, devices)
    leaving, cut = frame.chunks()

    own_cut, _ = frame.boundary(jnp.maximum(frame.shift, FIRST_ROWS))
    r1 = jnp.where(cut >= 0, cut, own_cut)
    e1, _ = frame.boundary(jnp.maximum(frame.shift, r1 + FIRST_ROWS), RB - W)
    e2, e2_a = frame.boundary(e1 + jnp.maximum(SECOND_ROWS - r1, 0), RB - W)
    tab[T_PHASE : T_PHASE + 1] = lanes([r1, e1, e2, e2_a])

    i = lane[:, :RB]
    a = frame.agg(i)
    first = frame.agg(i - W) - a + W
    slots = frame.agg(i + W) - a + W - first + 1
    goal = jnp.maximum(a - AD, 0) * KC
    for n, (second, place, low, count) in enumerate(leaving):
        block = jnp.where(second == 1, BASES[1], BASES[0]) + place - low
        goal = jnp.where(a == n, block, goal)
    tab[T_GOAL : T_GOAL + 1, :RB] = goal
    tab[T_HEAD : T_HEAD + 1, :RB] = first + 16 * slots + 256 * jnp.maximum(a - AD, 0)

    j_low = jnp.where(dev == 0, 0, -W)
    j_high = jnp.where(dev == devices - 1, RB, RB + W)
    k = lax.broadcasted_iota(jnp.int32, (K, RB), 0)
    j = lax.broadcasted_iota(jnp.int32, (K, RB), 1) + offs[...]
    ok = jnp.logical_and(k < counts[...], jnp.logical_and(j >= j_low, j < j_high))
    slot = jnp.where(ok, frame.agg(j) - a + W, SPARE)
    tab[:K, :RB] = slot * 256 + j + W


def edges_kernel(
    starts_hbm, offs_hbm, counts_hbm, a_hbm, p_hbm, av, win, blocks, tab,
    starts, offs, counts, send, recv, a_sems, sems,
):
    small = [
        pltpu.make_async_copy(src, dst, sems.at[n])
        for n, (src, dst) in enumerate(
            ((starts_hbm, starts), (offs_hbm, offs), (counts_hbm, counts))
        )
    ]
    parts = a_sems.shape[0]
    size = EARLY // parts
    local = [pltpu.make_async_copy(p_hbm, win.at[pl.ds(W, RB)], sems.at[3])]
    for n in range(parts):
        rows = pl.ds(n * size, size)
        local.append(pltpu.make_async_copy(a_hbm.at[rows], av.at[rows], a_sems.at[n]))

    dev, devices = position(), total()
    cores = lax.axis_size("sub")
    mesh = pl.DeviceIdType.MESH

    def device(d):
        return (lax.div(d, cores), lax.rem(d, cores))

    left, right = device(jnp.maximum(dev - 1, 0)), device(jnp.minimum(dev + 1, devices - 1))
    has_left, has_right = dev > 0, dev < devices - 1
    sides = ((has_left, left), (has_right, right))
    barrier = pltpu.get_barrier_semaphore()
    for has, other in sides:

        @pl.when(has)
        def _(other=other):
            pl.semaphore_signal(barrier, inc=1, device_id=other, device_id_type=mesh)

    for copy in small + local:
        copy.start()

    neighbours = has_left.astype(jnp.int32) + has_right.astype(jnp.int32)
    pl.semaphore_wait(barrier, neighbours)
    copies = [
        pltpu.make_async_remote_copy(
            src_ref=p_hbm.at[pl.ds(src, W)],
            dst_ref=win.at[pl.ds(dst, W)],
            send_sem=send.at[n],
            recv_sem=recv.at[n],
            device_id=other,
            device_id_type=mesh,
        )
        for n, src, dst, other in ((0, 0, RB + W, left), (1, RB - W, 0, right))
    ]
    for (has, _), copy in zip(sides, copies):
        pl.when(has)(copy.start)

    def clear(b, carry):
        for n in range(CLEAR):
            blocks[b * CLEAR + n] = jnp.zeros((B, B), F32)
        return carry

    lax.fori_loop(0, BLOCKS // CLEAR, clear, 0)
    for copy in small:
        copy.wait()
    fill_table(starts, offs, counts, tab)
    for copy in local:
        copy.wait()
    for (has, _), copy, at, arrival in zip(sides, copies, (0, RB + W), copies[::-1]):
        pl.when(has)(copy.wait_send)
        pl.when(has)(arrival.wait_recv)

        @pl.when(jnp.logical_not(has))
        def _(at=at):
            for n in range(W):
                win[at + n] = jnp.zeros((B, B), BF)


def edges_call(starts, offs, counts, a, p):
    vmem = pl.BlockSpec(memory_space=pltpu.VMEM)
    hbm = pl.BlockSpec(memory_space=pltpu.HBM)
    return pl.pallas_call(
        edges_kernel,
        out_shape=[
            jax.ShapeDtypeStruct((RB, K, B, B), BF),
            jax.ShapeDtypeStruct((RB + 2 * W, B, B), BF),
            jax.ShapeDtypeStruct((BLOCKS, B, B), F32),
            jax.ShapeDtypeStruct(TABLE, jnp.int32),
        ],
        in_specs=[hbm] * 5,
        out_specs=[vmem] * 4,
        scratch_shapes=[
            pltpu.SMEM(starts.shape, jnp.int32),
            pltpu.VMEM(offs.shape, jnp.int32),
            pltpu.VMEM(counts.shape, jnp.int32),
            pltpu.SemaphoreType.DMA((2,)),
            pltpu.SemaphoreType.DMA((2,)),
            pltpu.SemaphoreType.DMA((4,)),
            pltpu.SemaphoreType.DMA((4,)),
        ],
        compiler_params=pltpu.CompilerParams(
            collective_id=0, has_side_effects=True, vmem_limit_bytes=VMEM_LIMIT
        ),
        cost_estimate=pl.CostEstimate(flops=1000, bytes_accessed=20 << 20, transcendentals=0),
        name="edges",
    )(starts, offs, counts, a, p)


def received(tab, a):
    v = tab[T_RECV, a]
    n = jnp.bitwise_and(v, 15)
    low = jnp.bitwise_and(lax.shift_right_logical(v, 4), 15)
    place = jnp.bitwise_and(lax.shift_right_logical(v, 8), 63)
    return lax.shift_right_logical(v, 14), place, low, n


def phase_kernel(phase, *refs):
    refs = list(refs)
    tab_in, win, state, av = refs[:4]
    del refs[:4]
    a_hbm = refs.pop(0) if phase == 0 else None
    arrived = refs.pop(0) if phase == 2 else None
    blocks = refs.pop(0)
    extra = refs.pop(0)
    if phase == 0:
        av = refs.pop(0)
    out_hbm = refs.pop(0) if phase == 2 else None
    tab, *acc, tab_sem, out_sems, late_sems = refs
    del state

    def late_copy(n):
        rows = pl.ds(EARLY + n * PIECE, PIECE)
        return pltpu.make_async_copy(a_hbm.at[rows], av.at[rows], late_sems.at[n])

    def late_wait(n, carry):
        late_copy(n).wait()
        return carry

    late = (RB - EARLY) // PIECE
    if phase == 0:
        for n in range(late):
            late_copy(n).start()
    chunk = (1, 0, None)[phase]

    tab_copy = pltpu.make_async_copy(tab_in, tab, tab_sem)
    tab_copy.start()
    tab_copy.wait()
    r1, e1, e2, e2_a = [tab[T_PHASE, n] for n in range(4)]
    rows = (e1 - r1, r1 + e2 - e1, RB - e2)[phase]

    def row_at(t):
        if phase == 1:
            return t + jnp.where(t < r1, 0, e1 - r1)
        return t + (r1, 0, e2)[phase]

    def out_copy(a):
        return pltpu.make_async_copy(
            blocks.at[pl.ds(a * KC, KC)], out_hbm.at[a], out_sems.at[a]
        )

    def put(a, carry):
        out_copy(a).start()
        return carry

    def put_wait(a, carry):
        out_copy(a).wait()
        return carry

    if phase == 2:
        lax.fori_loop(0, e2_a, put, 0)

        def take(a, carry):
            which, place, low, n = received(tab, a)

            def one(s, carry):
                blocks[a * KC + low + s] = arrived[place + s].astype(F32)
                return carry

            lax.fori_loop(0, jnp.where(which == 1, n, 0), one, 0)
            return carry

        lax.fori_loop(e2_a, AD, take, 0)

        part = jnp.int32(AD - 1)
        for a in range(AD - 1, -1, -1):
            part = jnp.where(received(tab, a)[3] > 0, a, part)
        lax.fori_loop(part + 1, AD, put, 0)

    def group(g, done):
        if phase == 0:
            last = row_at(jnp.minimum(g * GROUP + GROUP, rows))
            need = lax.div(jnp.maximum(last - EARLY, 0) + (PIECE - 1), PIECE)
            done = lax.fori_loop(done, need, lambda n, c: late_wait(n, c + 1), done)
        places, firsts, goals = [], [], []
        span = jnp.int32(0)
        for u in range(GROUP):
            t = g * GROUP + u
            i = row_at(jnp.minimum(t, rows - 1))
            head = tab[T_HEAD, i]
            span = jnp.maximum(span, jnp.bitwise_and(lax.shift_right_logical(head, 4), 15))
            places.append(i)
            firsts.append(jnp.bitwise_and(head, 15))
            goals.append(jnp.where(t < rows, tab[T_GOAL, i], TRASH))

        def compute(slots):
            applied = []
            heads = [jnp.minimum(f, KC - slots) for f in firsts]
            for u in range(GROUP):
                for s in range(slots):
                    acc[u][heads[u] + s] = jnp.zeros((B, B), F32)
            for k in range(K):
                for u in range(GROUP):
                    i = places[u]
                    code = tab[k, i]
                    slot = lax.shift_right_logical(code, 8)
                    product = jnp.dot(
                        av[i, k],
                        win[jnp.bitwise_and(code, 255)],
                        preferred_element_type=F32,
                    )
                    acc[u][slot] = acc[u][slot] + product
            for u in range(GROUP):
                applied.append(
                    jnp.concatenate(
                        [acc[u][heads[u] + s].astype(BF) for s in range(slots)], axis=1
                    )
                )
            for u in range(GROUP):
                term = lax.dot_general(
                    win[places[u] + W],
                    applied[u],
                    (((0,), (0,)), ((), ())),
                    preferred_element_type=F32,
                )
                goal = goals[u] + heads[u]
                for s in range(slots):
                    blocks[goal + s] = blocks[goal + s] + term[:, s * B : (s + 1) * B]

        pl.when(span <= 3)(lambda: compute(3))
        pl.when(jnp.logical_and(span > 3, span <= 5))(lambda: compute(5))
        pl.when(span > 5)(lambda: compute(7))

        if phase < 2:
            return done
        t = (g + 1) * GROUP
        ahead = lax.shift_right_logical(tab[T_HEAD, row_at(jnp.minimum(t, rows - 1))], 8)
        ready = jnp.where(t < rows, ahead, done)
        return lax.fori_loop(done, jnp.maximum(ready, done), lambda a, c: put(a, c + 1), done)

    start = (0, 0, e2_a)[phase]
    done = lax.fori_loop(0, lax.div(rows + (GROUP - 1), GROUP), group, jnp.int32(start))
    if chunk is not None:
        for b in range(CHUNKS[chunk]):
            extra[b] = blocks[BASES[chunk] + b].astype(BF)
        if phase == 0:
            lax.fori_loop(done, late, late_wait, 0)
        return
    lax.fori_loop(done, part + 1, put, 0)
    for c in range(KC):
        extra[c] = blocks[part * KC + c]
    lax.fori_loop(0, AD, put_wait, 0)


def phase_call(phase, tab, win, blocks, a, more=()):
    vmem = pl.BlockSpec(memory_space=pltpu.VMEM)
    hbm = pl.BlockSpec(memory_space=pltpu.HBM)
    shapes = [jax.ShapeDtypeStruct((BLOCKS, B, B), F32)]
    in_specs = [vmem] * 4
    out_specs = [vmem, vmem]
    aliases = {2: 0}
    if phase == 2:
        shapes.append(jax.ShapeDtypeStruct((KC, B, B), F32))
        shapes.append(jax.ShapeDtypeStruct((AD, KC, B, B), F32))
        in_specs.append(vmem)
        out_specs.append(hbm)
    else:
        shapes.append(jax.ShapeDtypeStruct((CHUNKS[1 - phase], B, B), BF))
    if phase == 0:
        shapes.append(jax.ShapeDtypeStruct((RB, K, B, B), BF))
        in_specs.append(hbm)
        out_specs.append(vmem)
        aliases[3] = 2
    return pl.pallas_call(
        functools.partial(phase_kernel, phase),
        out_shape=shapes,
        in_specs=in_specs,
        out_specs=out_specs,
        scratch_shapes=[
            pltpu.SMEM(TABLE, jnp.int32),
            *[pltpu.VMEM((K, B, B), F32)] * GROUP,
            pltpu.SemaphoreType.DMA,
            pltpu.SemaphoreType.DMA((AD,)),
            pltpu.SemaphoreType.DMA(((RB - EARLY) // PIECE,)),
        ],
        input_output_aliases=aliases,
        compiler_params=pltpu.CompilerParams(vmem_limit_bytes=VMEM_LIMIT),
        cost_estimate=pl.CostEstimate(
            flops=1_500_000_000, bytes_accessed=8 << 20, transcendentals=0
        ),
        name=f"phase{phase}",
    )(tab, win, blocks, a, *more)


def final_kernel(tab_in, arrived, part, out_in, out_hbm, tab, blocks, sems, tab_sem):
    del out_in
    tab_copy = pltpu.make_async_copy(tab_in, tab, tab_sem)
    tab_copy.start()
    tab_copy.wait()

    def store(a, place, slot):
        return pltpu.make_async_copy(blocks.at[place], out_hbm.at[a, slot], sems.at[place])

    def each(act):
        def visit(a, seen):
            which, place, low, n = received(tab, a)

            def one(s, carry):
                act(a, place + s, low + s, seen)
                return carry

            lax.fori_loop(0, jnp.where(which == 0, n, 0), one, 0)
            return jnp.where(n > 0, 1, seen)

        lax.fori_loop(0, AD, visit, jnp.int32(0))

    def add(a, place, slot, seen):
        value = arrived[place].astype(F32)
        blocks[place] = jnp.where(seen == 0, value + part[slot], value)
        store(a, place, slot).start()

    each(add)
    each(lambda a, place, slot, seen: store(a, place, slot).wait())


def final_call(tab, arrived, part, out):
    vmem = pl.BlockSpec(memory_space=pltpu.VMEM)
    hbm = pl.BlockSpec(memory_space=pltpu.HBM)
    size = CHUNKS[0]
    return pl.pallas_call(
        final_kernel,
        out_shape=jax.ShapeDtypeStruct((AD, KC, B, B), F32),
        in_specs=[vmem, vmem, vmem, hbm],
        out_specs=hbm,
        scratch_shapes=[
            pltpu.SMEM(TABLE, jnp.int32),
            pltpu.VMEM((size, B, B), F32),
            pltpu.SemaphoreType.DMA((size,)),
            pltpu.SemaphoreType.DMA,
        ],
        input_output_aliases={3: 0},
        compiler_params=pltpu.CompilerParams(vmem_limit_bytes=VMEM_LIMIT),
        cost_estimate=pl.CostEstimate(flops=1_000_000, bytes_accessed=4 << 20, transcendentals=0),
        name="final",
    )(tab, arrived, part, out)


def shards(a_blocks, nbr_offset, nbr_count, prolong, owner_start):
    axes = ("dom", "sub")
    down = [(i + 1, i) for i in range(total() - 1)]
    inputs = (owner_start, nbr_offset.T, nbr_count.reshape(1, RB), a_blocks, prolong)
    inputs = [pltpu.with_memory_space_constraint(x, pltpu.HBM) for x in inputs]
    a, win, blocks, tab = edges_call(*inputs)
    blocks, pack_b, a = phase_call(0, tab, win, blocks, a, inputs[3:4])
    recv_b = lax.ppermute(pack_b, axes, down)
    blocks, pack_a = phase_call(1, tab, win, blocks, a)
    recv_a = lax.ppermute(pack_a, axes, down)
    blocks, part, out = phase_call(2, tab, win, blocks, a, (recv_b,))
    return final_call(tab, recv_a, part, out)


def solution(mesh):
    placed = (
        P(("dom", "sub"), None, None, None),
        P(("dom", "sub"), None),
        P(("dom", "sub")),
        P(("dom", "sub"), None, None),
        P(),
    )
    return jax.shard_map(
        shards,
        mesh=mesh,
        in_specs=placed,
        out_specs=P(("dom", "sub"), None, None, None),
        check_vma=False,
    )
```
